256 devices in a mesh: gz: 32 (over z, y_hi, core), col: 8 (over x, y_lo).
Axes of the slice: x: 4, y: 4 (y_hi: 2, y_lo: 2; y = y_hi * 2 + y_lo), z: 8, core: 2. Of those that a mesh axis runs over, the one named last changes fastest.
Arguments:
- features: bfloat16 [32, 512, 512], P('gz', 'col'), may hold values from -6 to 6
- filters: bfloat16 [3, 3, 3, 512, 512], P(None, None, None, 'col'), may hold values from -0.0546875 to 0.0546875
- cotangent: bfloat16 [32, 512, 512], P('gz', 'col'), may hold values from -6 to 6
Outputs:
- output: bfloat16 [32, 512, 512], P('gz', 'col')
- input_grad: bfloat16 [32, 512, 512], P('gz', 'col')
- filter_grad: float32 [3, 3, 3, 512, 512], P(None, None, None, 'col')
The draws below stay inside these ranges and needn't reach their ends.
All inputs are finite; a program needn't handle non-finite values.
Results may differ from the reference program's by a relative error of at most 0.0015.
Values may be sent and summed in bfloat16 or wider, within the bound.
No kernel may reach another device: no remote copies, remote signals or barrier semaphores. Data moves between devices by JAX's collectives and lax.ppermute only.
A program may use at most 128 MiB of HBM per device.

```python
import jax
import jax.numpy as jnp

C = 512
NY = 32
NZ = 16
NX = 32


def block_levels(stream_key, dims, cuts, smallest, high):
    loudness, own = 1.0, jax.random.fold_in(stream_key, 6)
    for position, blocks in cuts:
        steps = jnp.exp(jax.random.uniform(jax.random.fold_in(own, position), (blocks,), jnp.float32, smallest / len(cuts), high / len(cuts)))
        loudness = loudness * jnp.repeat(steps, dims[position] // blocks).reshape([-1 if axis == position else 1 for axis in range(len(dims))])
    return loudness


def centred(stream_key, shape, spread, limit, pieces=(), held_as=jnp.bfloat16):
    entries = spread * jax.random.normal(stream_key, shape, jnp.float32)
    if pieces:
        entries = entries * block_levels(stream_key, shape, pieces, -0.22, 0.18)
    return jnp.clip(entries, -limit, limit).astype(held_as)


def setup_inputs(seed: int = 0) -> dict:
    keys = jax.random.split(jax.random.key(seed), 4)
    features = centred(keys[0], (NX, C, NY * NZ), 1.0, 6.0, ((0, 32), (1, 8)))
    filters = centred(keys[1], (3, 3, 3, C, C), (27 * C) ** -0.5, 0.0546875, ((3, 8),))
    cotangent = centred(keys[2], (NX, C, NY * NZ), 1.0, 6.0, ((0, 32), (1, 8)))
    return {"features": features, "filters": filters, "cotangent": cotangent}


def reference(features, filters, cotangent):
    grid = features.reshape(NX, C, NY, NZ)
    cot_grid = cotangent.reshape(NX, C, NY, NZ)
    widths = ((1, 1), (0, 0), (1, 1), (1, 1))
    padded = jnp.pad(grid, widths)
    cot_padded = jnp.pad(cot_grid, widths)
    cot_wide = cot_grid.astype(jnp.float32)
    output = jnp.zeros((NX, C, NY, NZ), jnp.float32)
    input_grad = jnp.zeros((NX, C, NY, NZ), jnp.float32)
    grads = []
    for shift_x in range(3):
        for shift_y in range(3):
            for shift_z in range(3):
                tap = filters[shift_x, shift_y, shift_z].astype(jnp.float32)
                window = padded[shift_x:shift_x + NX, :, shift_y:shift_y + NY, shift_z:shift_z + NZ].astype(jnp.float32)
                output = output + jnp.einsum('on,xnyz->xoyz', tap, window)
                grads.append(jnp.einsum('xoyz,xnyz->on', cot_wide, window))
                moved = cot_padded[2 - shift_x:2 - shift_x + NX, :, 2 - shift_y:2 - shift_y + NY, 2 - shift_z:2 - shift_z + NZ].astype(jnp.float32)
                input_grad = input_grad + jnp.einsum('on,xoyz->xnyz', tap, moved)
    scale = 1.0 / jnp.sqrt(jnp.float32(NX * NY * NZ))
    filter_grad = jnp.stack(grads).reshape(3, 3, 3, C, C) * scale
    return (output.reshape(NX, C, NY * NZ).astype(jnp.bfloat16), input_grad.reshape(NX, C, NY * NZ).astype(jnp.bfloat16), filter_grad)
```

```python
import functools

import jax
import jax.numpy as jnp
from jax import lax
from jax.experimental import pallas as pl
from jax.experimental.pallas import tpu as pltpu
from jax.sharding import PartitionSpec as P

NY = 32
NZ = 16
VMEM = pl.BlockSpec(memory_space=pltpu.VMEM)


def shifted(value, down, right):
    cells = NY * NZ
    step = down * NZ + right
    if step:
        value = pltpu.roll(value, (-step) % cells, 1)
    cell = lax.broadcasted_iota(jnp.int32, value.shape, 1)
    row, col = cell // NZ, cell % NZ
    if down == 1:
        value = jnp.where(row < NY - 1, value, 0.0)
    if down == -1:
        value = jnp.where(row > 0, value, 0.0)
    if right == 1:
        value = jnp.where(col < NZ - 1, value, 0.0)
    if right == -1:
        value = jnp.where(col > 0, value, 0.0)
    return value


def spread_taps(cot, out_ref, base):
    outs = cot.shape[0]
    wide = cot.astype(jnp.float32)
    for tap in range(9):
        b, c = divmod(tap, 3)
        out_ref[base + tap * outs : base + (tap + 1) * outs, :] = shifted(wide, 1 - b, 1 - c).astype(jnp.bfloat16)


def input_kernel(cot_ref, taps_ref, out_ref, spread_ref):
    size = 9 * cot_ref.shape[1]
    for a in range(3):
        spread_taps(cot_ref[2 - a], spread_ref, a * size)
    out_ref[...] = lax.dot_general(
        taps_ref[...], spread_ref[...], (((0,), (0,)), ((), ())), preferred_element_type=jnp.float32
    )


def output_kernel(window_ref, taps_ref, out_ref, acc_ref):
    size = acc_ref.shape[0]
    for a in range(3):
        part = jnp.dot(taps_ref[a * size : (a + 1) * size, :], window_ref[a], preferred_element_type=jnp.float32)
        if a:
            acc_ref[...] += part
        else:
            acc_ref[...] = part
    outs = size // 9
    total = jnp.zeros((outs, NY * NZ), jnp.float32)
    for tap in range(9):
        b, c = divmod(tap, 3)
        total = total + shifted(acc_ref[tap * outs : (tap + 1) * outs, :], b - 1, c - 1)
    out_ref[...] = total.astype(jnp.bfloat16)


def filter_kernel(cot_ref, window_ref, out_ref, spread_ref):
    for q in range(4):
        spread_taps(cot_ref[q], spread_ref, 0)
        part = lax.dot_general(
            spread_ref[...], window_ref[q], (((1,), (1,)), ((), ())), preferred_element_type=jnp.float32
        )
        if q:
            out_ref[...] += part
        else:
            out_ref[...] = part


def call(kernel, out, scratch, flops, *args):
    return pl.pallas_call(
        kernel,
        out_shape=out,
        in_specs=[VMEM] * len(args),
        out_specs=VMEM,
        scratch_shapes=[scratch],
        compiler_params=pltpu.CompilerParams(vmem_limit_bytes=48 << 20),
        cost_estimate=pl.CostEstimate(
            flops=flops, transcendentals=0, bytes_accessed=sum(a.size * a.dtype.itemsize for a in args)
        ),
    )(*args)


def body(features, filters, cotangent):
    _, local, cells = features.shape
    devices = lax.axis_size("gz")
    cols = lax.axis_size("col")
    channels = local * cols
    quads = devices // 4
    place = lax.axis_index("gz")
    core = place % 2
    spot = place % 4
    x_own = features[0]
    c_own = cotangent[0]

    def xor(value, bits):
        return lax.ppermute(value, "gz", [(i, i ^ bits) for i in range(devices)])

    outward = [(i, i + 1) for i in range(1, devices - 1, 2)] + [(i, i - 1) for i in range(2, devices, 2)]

    def everywhere(block, axis, groups=None):
        count = len(groups[0]) if groups else lax.axis_size(axis)
        copies = jnp.broadcast_to(block[None], (count,) + block.shape)
        return lax.all_to_all(copies, axis, 0, 0, axis_index_groups=groups, tiled=True)

    x_halo = lax.ppermute(x_own, "gz", outward)
    c_halo = lax.ppermute(c_own, "gz", outward)
    own = everywhere(x_own, "col").reshape(channels, cells)
    halo = everywhere(x_halo, "col").reshape(channels, cells)
    other = xor(own, 1)
    half = channels // 2
    quarter = channels // 4
    other_halo = xor(lax.dynamic_slice_in_dim(halo, (1 - core) * half, half, 0), 1)
    first = core == 0
    side = spot // 2
    turn = 2 * core + side

    four = [[4 * g + r for r in range(4)] for g in range(quads)]
    c_quad = everywhere(c_own, "gz", four)
    c_other = xor(c_own, 1)
    c_three = jnp.where(first, jnp.stack([c_halo, c_own, c_other]), jnp.stack([c_other, c_own, c_halo]))

    tops = jnp.stack([jnp.max(jnp.abs(own)), jnp.max(jnp.abs(c_own))]).astype(jnp.float32)
    tops = everywhere(jnp.broadcast_to(tops[:, None], (2, 128)), "gz")
    tops = jnp.max(tops, axis=(0, 2))
    total_cells = cells * devices
    scale = 1.0 / jnp.sqrt(jnp.float32(total_cells))
    bound = jnp.maximum(tops[0] * tops[1] * (total_cells * scale), 1e-25)
    up = 30000.0 / bound
    down = bound * (1.0 / 30000.0)

    taps = filters.reshape(27 * local, channels)
    size = 9 * local
    flops = 2 * 27 * local * channels * cells

    partial = call(
        input_kernel,
        jax.ShapeDtypeStruct((channels, cells), jnp.float32),
        pltpu.VMEM((3 * size, cells), jnp.bfloat16),
        flops,
        c_three,
        taps,
    )
    pieces = lax.all_to_all(partial.reshape(cols, local, cells), "col", 0, 0, tiled=True)
    input_grad = jnp.sum(pieces, axis=0).astype(jnp.bfloat16)[None]

    window = jnp.where(first, jnp.stack([halo, own, other]), jnp.stack([other, own, halo]))
    output = call(
        output_kernel,
        jax.ShapeDtypeStruct((local, cells), jnp.bfloat16),
        pltpu.VMEM((size, cells), jnp.float32),
        flops,
        window,
        taps,
    )[None]

    def cut(value, index, width):
        return lax.dynamic_slice_in_dim(value, index * width, width, 0)

    own_first = jnp.where(first, own, other)
    own_last = jnp.where(first, other, own)
    far = xor(cut(jnp.where(spot < 2, own_first, own_last), turn ^ 1, quarter), 2)
    halo_half = cut(halo, core, half)
    halo_first = jnp.where(first, halo_half, other_halo)
    halo_last = jnp.where(first, other_halo, halo_half)
    outer = [halo_first, cut(own_first, core, half), cut(own_last, core, half), halo_last]
    own_first, own_last = cut(own_first, turn, quarter), cut(own_last, turn, quarter)
    near_last = cut(halo_last, side, quarter)
    near_first = cut(halo_first, side, quarter)
    inner = [
        jnp.where(side == 0, own_first, far),
        jnp.where(side == 0, own_last, near_first),
        jnp.where(side == 0, near_last, own_first),
        jnp.where(side == 0, far, own_last),
    ]
    windows = jnp.stack([jnp.concatenate([a, b], axis=0) for a, b in zip(outer, inner)])
    width = half + quarter
    grads = call(
        filter_kernel,
        jax.ShapeDtypeStruct((size, width), jnp.float32),
        pltpu.VMEM((size, cells), jnp.bfloat16),
        flops,
        c_quad,
        windows,
    )
    ring = [[4 * g + r for g in range(quads)] for r in range(4)]
    narrow = (grads * (scale * up)).astype(jnp.float16).reshape(quads, size // quads, width)
    narrow = lax.all_to_all(narrow, "gz", 0, 0, axis_index_groups=ring, tiled=True)
    mine = jnp.sum(narrow.astype(jnp.float32), axis=0).astype(jnp.float16)
    mine = everywhere(mine, "gz", ring).reshape(size, width)
    beyond = xor(mine, 2)
    both = jnp.stack([mine, beyond])
    swapped = xor(both, 1)
    low = jnp.where(first, both, swapped)
    high = jnp.where(first, swapped, both)
    low = jnp.where(side == 0, low, low[::-1])
    high = jnp.where(side == 0, high, high[::-1])
    offset0 = jnp.concatenate([low[0][:, :half], high[0][:, :half]], axis=1)
    offset1 = jnp.concatenate([low[0][:, half:], low[1][:, half:], high[0][:, half:], high[1][:, half:]], axis=1)
    offset2 = jnp.concatenate([low[1][:, :half], high[1][:, :half]], axis=1)
    filter_grad = jnp.stack([offset0, offset1, offset2]).astype(jnp.float32) * down
    return output, input_grad, filter_grad.reshape(3, 3, 3, local, channels)


def solution(mesh):
    in_specs = (P("gz", "col", None), P(None, None, None, "col", None), P("gz", "col", None))
    out_specs = (P("gz", "col", None), P("gz", "col", None), P(None, None, None, "col", None))
    return jax.shard_map(body, mesh=mesh, in_specs=in_specs, out_specs=out_specs, check_vma=False)
```

```python
import jax
import jax.numpy as jnp
from jax import lax
from jax.experimental import pallas as pl
from jax.experimental.pallas import tpu as pltpu
from jax.sharding import PartitionSpec as P

NY = 32
NZ = 16
VMEM = pl.BlockSpec(memory_space=pltpu.VMEM)
SMEM = pl.BlockSpec(memory_space=pltpu.SMEM)
LOG2 = 0.6931471805599453
TOP = 13.0
EXTRA = 8


def shifted(value, down, right):
    cells = NY * NZ
    step = down * NZ + right
    if step:
        value = pltpu.roll(value, (-step) % cells, 1)
    cell = lax.broadcasted_iota(jnp.int32, value.shape, 1)
    row, col = cell // NZ, cell % NZ
    if down == 1:
        value = jnp.where(row < NY - 1, value, 0.0)
    if down == -1:
        value = jnp.where(row > 0, value, 0.0)
    if right == 1:
        value = jnp.where(col < NZ - 1, value, 0.0)
    if right == -1:
        value = jnp.where(col > 0, value, 0.0)
    return value


def spread_taps(cot_ref, out_ref):
    outs = cot_ref.shape[0]
    wide = cot_ref[...].astype(jnp.float32)
    for tap in range(9):
        b, c = divmod(tap, 3)
        out_ref[tap * outs : (tap + 1) * outs, :] = shifted(wide, 1 - b, 1 - c).astype(jnp.bfloat16)


def lines(ref, first, count, beyond=False):
    _, both, cells = ref.shape
    local = both // 2
    return ref[pl.ds(first, count), (local if beyond else 0) : (both if beyond else local), :].reshape(count * local, cells)


def input_kernel(spot_ref, col_ref, halo_ref, own_ref, other_ref, taps_ref, *refs):
    out_refs, (spread_ref, acc_ref) = refs[:-2], refs[-2:]
    away = 2 - 2 * (spot_ref[0] % 2)
    spread_taps(halo_ref, spread_ref.at[0])
    spread_taps(own_ref, spread_ref.at[1])
    spread_taps(other_ref, spread_ref.at[2])

    def part(a, source):
        return lax.dot_general(
            taps_ref[a], spread_ref[source], (((0,), (0,)), ((), ())), preferred_element_type=jnp.float32
        )

    acc_ref[...] = part(away, 0)
    acc_ref[...] += part(1, 1)
    acc_ref[...] += part(2 - away, 2)
    local = out_refs[0].shape[0]
    col = col_ref[0]
    for bits, out_ref in enumerate(out_refs):
        out_ref[...] = acc_ref[pl.ds(pl.multiple_of((col ^ bits) * local, local), local), :]


def output_kernel(spot_ref, mine_ref, other_ref, taps_ref, out_ref, acc_ref):
    away = 2 * (spot_ref[0] % 2)
    cols = mine_ref.shape[0]
    acc_ref[...] = jnp.dot(taps_ref[away], lines(mine_ref, 0, cols, True), preferred_element_type=jnp.float32)
    acc_ref[...] += jnp.dot(taps_ref[1], lines(mine_ref, 0, cols), preferred_element_type=jnp.float32)
    acc_ref[...] += jnp.dot(taps_ref[2 - away], lines(other_ref, 0, cols), preferred_element_type=jnp.float32)
    outs = acc_ref.shape[0] // 9
    total = jnp.zeros((outs, NY * NZ), jnp.float32)
    for tap in range(9):
        b, c = divmod(tap, 3)
        total = total + shifted(acc_ref[tap * outs : (tap + 1) * outs, :], b - 1, c - 1)
    out_ref[...] = total.astype(jnp.bfloat16)


def exponent(value):
    top = jnp.max(jnp.max(jnp.abs(value), axis=1, keepdims=True), axis=0, keepdims=True)
    top = jnp.broadcast_to(jnp.maximum(top, 1e-30), (1, value.shape[1]))
    return jnp.floor(jnp.log(top) * (1.0 / LOG2))


def filter_kernel(
    spot_ref, mine_ref, other_ref, far_ref, corner_ref, c0_ref, c1_ref, c2_ref, c3_ref, out_ref, window_ref, spread_ref, acc_ref
):
    spot = spot_ref[0]
    core, side = spot % 2, spot // 2
    turn = 2 * core + side
    cols = mine_ref.shape[0]
    half, quarter = cols // 2, cols // 4
    edge = acc_ref.shape[1] * 2 // 3
    window_ref[1 + core, :edge, :] = lines(mine_ref, core * half, half)
    window_ref[2 - core, :edge, :] = lines(other_ref, core * half, half)
    window_ref[3 * core, :edge, :] = lines(mine_ref, core * half, half, True)
    window_ref[3 - 3 * core, :edge, :] = lines(other_ref, core * half, half, True)
    window_ref[spot, edge:, :] = lines(mine_ref, turn * quarter, quarter)
    window_ref[spot + 1 - 2 * core, edge:, :] = lines(other_ref, turn * quarter, quarter)
    inside = core + side == 1

    @pl.when(inside)
    def _():
        window_ref[2 - side, edge:, :] = lines(mine_ref, turn * quarter, quarter, True)
        window_ref[3 - 3 * side, edge:, :] = far_ref[...].reshape(far_ref.shape[0] * far_ref.shape[1], -1)

    @pl.when(jnp.logical_not(inside))
    def _():
        window_ref[2 - side, edge:, :] = lines(other_ref, turn * quarter, quarter, True)
        window_ref[3 - 3 * side, edge:, :] = corner_ref[...].reshape(far_ref.shape[0] * far_ref.shape[1], -1)

    for d, cot_ref in enumerate((c0_ref, c1_ref, c2_ref, c3_ref)):
        place = spot
        if d % 2:
            place = place + 1 - 2 * core
        if d // 2:
            place = place + 2 - 4 * side
        spread_taps(cot_ref, spread_ref)
        part = lax.dot_general(
            spread_ref[...], window_ref[place], (((1,), (1,)), ((), ())), preferred_element_type=jnp.float32
        )
        if d:
            acc_ref[...] += part
        else:
            acc_ref[...] = part
    value = acc_ref[...]
    level = exponent(value)
    factor = jnp.exp((TOP - level) * LOG2)
    blocks, rows, width = out_ref.shape
    rows = rows - EXTRA
    for block in range(blocks):
        out_ref[block, :rows, :] = acc_ref[block * rows : (block + 1) * rows, :] * factor
        out_ref[block, rows:, :] = jnp.broadcast_to(level, (EXTRA, width))


def sum_kernel(in_ref, out_ref):
    blocks, rows, width = in_ref.shape
    rows = rows - EXTRA
    total = jnp.zeros((rows, width), jnp.float32)
    for block in range(blocks):
        total = total + in_ref[block, :rows, :] * jnp.exp((in_ref[block, rows : rows + 1, :] - TOP) * LOG2)
    level = exponent(total)
    out_ref[:rows, :] = total * jnp.exp((TOP - level) * LOG2)
    out_ref[rows:, :] = jnp.broadcast_to(level, (EXTRA, width))


def join_kernel(scale, spot_ref, p0_ref, p1_ref, p2_ref, p3_ref, out_ref):
    spot = spot_ref[0]
    core, side = spot % 2, spot // 2
    blocks, rows, width = p0_ref.shape
    rows = rows - EXTRA
    quarter = width // 3
    half = 2 * quarter
    for d, piece_ref in enumerate((p0_ref, p1_ref, p2_ref, p3_ref)):
        its_core = 1 - core if d % 2 else core
        its_side = 1 - side if d // 2 else side
        wide = pl.ds(pl.multiple_of(its_core * half, half), half)
        fine = pl.ds(pl.multiple_of((2 * its_core + its_side) * quarter, quarter), quarter)
        for block in range(blocks):
            down = jnp.exp((piece_ref[block, rows : rows + 1, :] - TOP) * LOG2) * scale
            value = piece_ref[block, :rows, :] * down
            lines = slice(block * rows, (block + 1) * rows)
            out_ref[2 * its_side, lines, wide] = value[:, :half]
            out_ref[1, lines, fine] = value[:, half:]


def call(kernel, out, scratch, flops, *args):
    return pl.pallas_call(
        kernel,
        out_shape=out,
        in_specs=[SMEM if a.dtype == jnp.int32 else VMEM for a in args],
        out_specs=[VMEM] * len(out) if isinstance(out, list) else VMEM,
        scratch_shapes=scratch,
        compiler_params=pltpu.CompilerParams(vmem_limit_bytes=48 << 20),
        cost_estimate=pl.CostEstimate(
            flops=flops, transcendentals=0, bytes_accessed=sum(a.size * a.dtype.itemsize for a in args)
        ),
    )(*args)


def body(features, filters, cotangent):
    _, local, cells = features.shape
    devices = lax.axis_size("gz")
    cols = lax.axis_size("col")
    channels = local * cols
    quads = devices // 4
    half = channels // 2
    quarter = channels // 4
    size = 9 * local
    width = half + quarter
    flops = 2 * 27 * local * channels * cells
    bf16, f16, f32 = jnp.bfloat16, jnp.float16, jnp.float32
    spot = lax.axis_index("gz") % 4
    core, side = spot % 2, spot // 2
    spots = spot.reshape(1)
    x_own = features[0]
    c_own = cotangent[0]
    taps = filters.reshape(3, size, channels)

    def xor(value, bits):
        return lax.ppermute(value, "gz", [(i, i ^ bits) for i in range(devices)])

    outward = [(i, i + 1) for i in range(1, devices - 1, 2)] + [(i, i - 1) for i in range(2, devices, 2)]
    ring = [[4 * g + r for g in range(quads)] for r in range(4)]

    def everywhere(block, axis, groups=None):
        count = len(groups[0]) if groups else lax.axis_size(axis)
        copies = jnp.broadcast_to(block[None], (count,) + block.shape)
        return lax.all_to_all(copies, axis, 0, 0, axis_index_groups=groups, tiled=True)

    x_halo = lax.ppermute(x_own, "gz", outward)
    c_other = xor(c_own, 1)
    c_across = xor(c_own, 2)
    c_corner = xor(c_own, 3)
    c_halo = lax.ppermute(c_own, "gz", outward)
    x_halo, c_other, c_across, c_corner, c_halo = lax.optimization_barrier((x_halo, c_other, c_across, c_corner, c_halo))
    gathered = everywhere(jnp.concatenate([x_own, x_halo]), "col")
    other = xor(gathered, 1)

    def quarter_of(turn):
        return lax.dynamic_slice(gathered, (turn * (cols // 4), 0, 0), (cols // 4, local, cells))

    last = side
    straight = [(4 * g, 4 * g + 2) for g in range(quads)] + [(4 * g + 3, 4 * g + 1) for g in range(quads)]
    across = [(4 * g, 4 * g + 3) for g in range(quads)] + [(4 * g + 3, 4 * g) for g in range(quads)]
    far = lax.ppermute(quarter_of(jnp.where(last == 1, 2, 1)), "gz", straight)
    corner = lax.ppermute(quarter_of(jnp.where(last == 1, 0, 3)), "gz", across)

    grads = call(
        filter_kernel,
        jax.ShapeDtypeStruct((quads, size // quads + EXTRA, width), f32),
        [pltpu.VMEM((4, width, cells), bf16), pltpu.VMEM((size, cells), bf16), pltpu.VMEM((size, width), f32)],
        flops,
        spots,
        gathered,
        other,
        far,
        corner,
        c_own,
        c_other,
        c_across,
        c_corner,
    )
    grads, c_halo, other = lax.optimization_barrier((grads, c_halo, other))
    narrow = lax.all_to_all(grads.astype(f16), "gz", 0, 0, axis_index_groups=ring, tiled=True)

    partial = call(
        input_kernel,
        [jax.ShapeDtypeStruct((local, cells), f32)] * cols,
        [pltpu.VMEM((3, size, cells), bf16), pltpu.VMEM((channels, cells), f32)],
        flops,
        spots,
        lax.axis_index("col").reshape(1),
        c_halo,
        c_own,
        c_other,
        taps,
    )

    def exchanged(bits, value):
        return lax.ppermute(value, "col", [(j, j ^ bits) for j in range(cols)])

    early = cols // 2
    pieces = [partial[0]] + [exchanged(bits, partial[bits]) for bits in range(1, early)]
    output = call(
        output_kernel,
        jax.ShapeDtypeStruct((local, cells), bf16),
        [pltpu.VMEM((size, cells), f32)],
        flops,
        spots,
        gathered,
        other,
        taps,
    )

    narrow, output, pieces, late = lax.optimization_barrier((narrow, output, pieces, partial[early:]))
    pieces = pieces + [exchanged(early + i, value) for i, value in enumerate(late)]
    mine = call(
        sum_kernel,
        jax.ShapeDtypeStruct((size // quads + EXTRA, width), f32),
        [],
        0,
        narrow.astype(f32),
    )
    mine = everywhere(mine.astype(f16), "gz", ring)
    input_grad = sum(pieces[1:], pieces[0]).astype(bf16)
    mine, input_grad = lax.optimization_barrier((mine, input_grad))
    across = xor(mine, 2)
    beside = xor(mine, 1)
    corner = xor(across, 1)
    scale = float((cells * devices) ** -0.5)

    def kernel(*refs):
        join_kernel(scale, *refs)

    filter_grad = call(
        kernel,
        jax.ShapeDtypeStruct((3, size, channels), f32),
        [],
        0,
        spots,
        mine.astype(f32),
        beside.astype(f32),
        across.astype(f32),
        corner.astype(f32),
    )
    return output[None], input_grad[None], filter_grad.reshape(3, 3, 3, local, channels)


def solution(mesh):
    in_specs = (P("gz", "col", None), P(None, None, None, "col", None), P("gz", "col", None))
    out_specs = (P("gz", "col", None), P("gz", "col", None), P(None, None, None, "col", None))
    return jax.shard_map(body, mesh=mesh, in_specs=in_specs, out_specs=out_specs, check_vma=False)
```

```python
import jax
import jax.numpy as jnp
from jax import lax
from jax.experimental import pallas as pl
from jax.experimental.pallas import tpu as pltpu
from jax.sharding import PartitionSpec as P

NY = 32
NZ = 16
VMEM = pl.BlockSpec(memory_space=pltpu.VMEM)
SMEM = pl.BlockSpec(memory_space=pltpu.SMEM)
LOG2 = 0.6931471805599453
TOP = 13.0
EXTRA = 8
LANES = 128


def shifted(value, down, right):
    cells = NY * NZ
    step = down * NZ + right
    if step:
        value = pltpu.roll(value, (-step) % cells, 1)
    cell = lax.broadcasted_iota(jnp.int32, value.shape, 1)
    row, col = cell // NZ, cell % NZ
    if down == 1:
        value = jnp.where(row < NY - 1, value, 0.0)
    if down == -1:
        value = jnp.where(row > 0, value, 0.0)
    if right == 1:
        value = jnp.where(col < NZ - 1, value, 0.0)
    if right == -1:
        value = jnp.where(col > 0, value, 0.0)
    return value


def spread_taps(cot_ref, out_ref):
    outs = cot_ref.shape[0]
    wide = cot_ref[...].astype(jnp.float32)
    for tap in range(9):
        b, c = divmod(tap, 3)
        out_ref[tap * outs : (tap + 1) * outs, :] = shifted(wide, 1 - b, 1 - c).astype(jnp.bfloat16)


def lines(ref, first, count, beyond=False):
    _, both, cells = ref.shape
    local = both // 2
    start = local if beyond else 0
    return ref[pl.ds(first, count), start : start + local, :].reshape(count * local, cells)


def pack_kernel(x_ref, c_ref, beyond_ref, across_ref, send_ref, here_ref):
    blocks, both, _ = send_ref.shape
    local = both // 2
    for block in range(blocks):
        send_ref[block, :local, :] = x_ref[...]
        send_ref[block, local:, :] = beyond_ref[0]
    here_ref[0] = c_ref[...]
    here_ref[1] = beyond_ref[1]
    here_ref[2] = across_ref[...]


def input_kernel(info_ref, here_ref, there_ref, taps_ref, give_ref, keep_ref, spread_ref, acc_ref):
    away = 2 - 2 * (info_ref[0] % 2)
    spread_taps(here_ref.at[0], spread_ref.at[0])
    spread_taps(here_ref.at[1], spread_ref.at[1])
    spread_taps(there_ref.at[0], spread_ref.at[2])

    def part(a, source):
        return lax.dot_general(
            taps_ref[a], spread_ref[source], (((0,), (0,)), ((), ())), preferred_element_type=jnp.float32
        )

    acc_ref[...] = part(1, 0)
    acc_ref[...] += part(2 - away, 2)

    @pl.when(info_ref[1] == 0)
    def _():
        acc_ref[...] += part(away, 1)

    count, local, _ = keep_ref.shape
    col = info_ref[3]
    for i in range(count):
        keep_ref[i] = acc_ref[pl.ds(pl.multiple_of((col ^ (2 * i)) * local, local), local), :]
        give_ref[i] = acc_ref[pl.ds(pl.multiple_of((col ^ (2 * i + 1)) * local, local), local), :]


def output_kernel(info_ref, mine_ref, other_ref, taps_ref, out_ref, acc_ref):
    away = 2 * (info_ref[0] % 2)
    cols = mine_ref.shape[0]
    acc_ref[...] = jnp.dot(taps_ref[1], lines(mine_ref, 0, cols), preferred_element_type=jnp.float32)
    acc_ref[...] += jnp.dot(taps_ref[2 - away], lines(other_ref, 0, cols), preferred_element_type=jnp.float32)

    @pl.when(info_ref[1] == 0)
    def _():
        acc_ref[...] += jnp.dot(taps_ref[away], lines(mine_ref, 0, cols, True), preferred_element_type=jnp.float32)

    outs = acc_ref.shape[0] // 9
    total = jnp.zeros((outs, NY * NZ), jnp.float32)
    for tap in range(9):
        b, c = divmod(tap, 3)
        total = total + shifted(acc_ref[tap * outs : (tap + 1) * outs, :], b - 1, c - 1)
    out_ref[...] = total.astype(jnp.bfloat16)


def exponent(value):
    top = jnp.max(jnp.max(jnp.abs(value), axis=1, keepdims=True), axis=0, keepdims=True)
    top = jnp.broadcast_to(jnp.maximum(top, 1e-30), (1, LANES))
    return jnp.floor(jnp.log(top) * (1.0 / LOG2))


def filter_kernel(info_ref, mine_ref, other_ref, here_ref, there_ref, out_ref, window_ref, far_ref, spread_ref, acc_ref):
    core, side = info_ref[0] % 2, info_ref[0] // 2
    turn = 2 * core + side
    cols = mine_ref.shape[0]
    half, quarter = cols // 2, cols // 4
    width = acc_ref.shape[1]
    edge = 2 * width // 3
    for slab, ref, beyond in (
        (1 + core, mine_ref, False),
        (2 - core, other_ref, False),
        (3 * core, mine_ref, True),
        (3 - 3 * core, other_ref, True),
    ):
        window_ref[slab + 1 - side, :edge, :] = lines(ref, core * half, half, beyond)
        window_ref[slab + side, edge:, :] = lines(ref, turn * quarter, quarter, beyond)
    zeros = jnp.zeros((edge, window_ref.shape[2]), window_ref.dtype)
    window_ref[4 * side, :edge, :] = zeros
    window_ref[4 - 4 * side, edge:, :] = zeros[: width - edge]

    @pl.when(info_ref[2] == 1)
    def _():
        window_ref[1 + 2 * side, :edge, :] = zeros

    inside = core + side == 1

    @pl.when(inside)
    def _():
        far_ref[...] = here_ref[2]

    @pl.when(jnp.logical_not(inside))
    def _():
        far_ref[...] = there_ref[2]

    for index, (at, cot_ref) in enumerate(
        (
            (side + 1 + core, here_ref.at[0]),
            (side + 3 * core, here_ref.at[1]),
            (side + 2 - core, there_ref.at[0]),
            (side + 3 - 3 * core, there_ref.at[1]),
            (4 - 4 * side, far_ref),
        )
    ):
        spread_taps(cot_ref, spread_ref)
        part = lax.dot_general(
            spread_ref[...], window_ref[at], (((1,), (1,)), ((), ())), preferred_element_type=jnp.float32
        )
        if index:
            acc_ref[...] += part
        else:
            acc_ref[...] = part
    level = exponent(acc_ref[...])
    factor = jnp.exp((TOP - level) * LOG2)
    blocks, height, _ = out_ref.shape
    tiles = width // LANES
    rows = (height - EXTRA) // tiles
    for block in range(blocks):
        for tile in range(tiles):
            part = acc_ref[block * rows : (block + 1) * rows, tile * LANES : (tile + 1) * LANES]
            out_ref[block, tile * rows : (tile + 1) * rows, :] = part * factor
        out_ref[block, height - EXTRA :, :] = jnp.broadcast_to(level, (EXTRA, LANES))


def sum_kernel(in_ref, out_ref):
    blocks, height, _ = in_ref.shape
    height = height - EXTRA
    total = jnp.zeros((height, LANES), jnp.float32)
    for block in range(blocks):
        total = total + in_ref[block, :height, :] * jnp.exp((in_ref[block, height : height + 1, :] - TOP) * LOG2)
    level = exponent(total)
    out_ref[:height, :] = total * jnp.exp((TOP - level) * LOG2)
    out_ref[height:, :] = jnp.broadcast_to(level, (EXTRA, LANES))


def join_kernel(scale, spot_ref, own_ref, other_ref, out_ref):
    core = spot_ref[0] % 2
    blocks, height, _ = own_ref.shape
    height = height - EXTRA
    tiles = 3 * out_ref.shape[2] // (4 * LANES)
    rows = height // tiles
    wide = 2 * tiles // 3
    for its_core, piece_ref in ((core, own_ref), (1 - core, other_ref)):
        for block in range(blocks):
            index, side = divmod(block, 2)
            down = jnp.exp((piece_ref[block, height : height + 1, :] - TOP) * LOG2) * scale
            span = slice(index * rows, (index + 1) * rows)
            for tile in range(tiles):
                value = piece_ref[block, tile * rows : (tile + 1) * rows, :] * down
                if tile < wide:
                    offset, at = 2 * side, its_core * wide + tile
                else:
                    offset, at = 1, (2 * its_core + side) * (tiles - wide) + tile - wide
                out_ref[offset, span, pl.ds(pl.multiple_of(at * LANES, LANES), LANES)] = value


def call(kernel, out, scratch, flops, *args):
    return pl.pallas_call(
        kernel,
        out_shape=out,
        in_specs=[SMEM if a.dtype == jnp.int32 else VMEM for a in args],
        out_specs=[VMEM] * len(out) if isinstance(out, list) else VMEM,
        scratch_shapes=scratch,
        compiler_params=pltpu.CompilerParams(vmem_limit_bytes=24 << 20),
        cost_estimate=pl.CostEstimate(
            flops=flops, transcendentals=0, bytes_accessed=sum(a.size * a.dtype.itemsize for a in args)
        ),
    )(*args)


def body(features, filters, cotangent):
    _, local, cells = features.shape
    devices = lax.axis_size("gz")
    cols = lax.axis_size("col")
    channels = local * cols
    quads = devices // 4
    half = channels // 2
    quarter = channels // 4
    size = 9 * local
    width = half + quarter
    height = size // quads * (width // LANES) + EXTRA
    flops = 2 * 27 * local * channels * cells
    bf16, f16, f32 = jnp.bfloat16, jnp.float16, jnp.float32
    place = lax.axis_index("gz")
    last = devices - 1
    info = jnp.stack(
        [
            place % 4,
            ((place == 0) | (place == last)).astype(jnp.int32),
            ((place < 2) | (place > last - 2)).astype(jnp.int32),
            lax.axis_index("col"),
        ]
    ).astype(jnp.int32)
    x_own = features[0]
    c_own = cotangent[0]
    taps = filters.reshape(3, size, channels)

    def xor(value, bits):
        return lax.ppermute(value, "gz", [(i, i ^ bits) for i in range(devices)])

    outward = [(i, (i + 1) % devices if i % 2 else (i - 1) % devices) for i in range(devices)]
    ring = [[4 * g + r for g in range(quads)] for r in range(4)]

    def everywhere(block, axis, groups=None):
        count = len(groups[0]) if groups else lax.axis_size(axis)
        copies = jnp.broadcast_to(block[None], (count,) + block.shape)
        return lax.all_to_all(copies, axis, 0, 0, axis_index_groups=groups, tiled=True)

    beyond = lax.ppermute(jnp.stack([x_own, c_own]), "gz", outward)
    across = xor(c_own, 2)
    send, here = call(
        pack_kernel,
        [jax.ShapeDtypeStruct((cols, 2 * local, cells), bf16), jax.ShapeDtypeStruct((3, local, cells), bf16)],
        [],
        0,
        x_own,
        c_own,
        beyond,
        across,
    )
    gathered = lax.all_to_all(send, "col", 0, 0, tiled=True)
    there = xor(here, 1)

    give, keep = call(
        input_kernel,
        [jax.ShapeDtypeStruct((cols // 2, local, cells), f32)] * 2,
        [pltpu.VMEM((3, size, cells), bf16), pltpu.VMEM((channels, cells), f32)],
        flops,
        info,
        here,
        there,
        taps,
    )
    gathered, there, give, keep = lax.optimization_barrier((gathered, there, give, keep))
    other = xor(gathered, 1)

    grads = call(
        filter_kernel,
        jax.ShapeDtypeStruct((quads, height, LANES), f32),
        [
            pltpu.VMEM((5, width, cells), bf16),
            pltpu.VMEM((local, cells), bf16),
            pltpu.VMEM((size, cells), bf16),
            pltpu.VMEM((size, width), f32),
        ],
        flops,
        info,
        gathered,
        other,
        here,
        there,
    )
    grads, give, other = lax.optimization_barrier((grads, give, other))
    narrow = lax.all_to_all(grads.astype(f16), "gz", 0, 0, axis_index_groups=ring, tiled=True)

    def exchanged(bits, value):
        return lax.ppermute(value, "col", [(j, j ^ bits) for j in range(cols)])

    given = exchanged(1, give)
    output = call(
        output_kernel,
        jax.ShapeDtypeStruct((local, cells), bf16),
        [pltpu.VMEM((size, cells), f32)],
        flops,
        info,
        gathered,
        other,
        taps,
    )

    narrow, output, given = lax.optimization_barrier((narrow, output, given))
    mine = call(
        sum_kernel,
        jax.ShapeDtypeStruct((height, LANES), f32),
        [],
        0,
        narrow.astype(f32),
    )
    both = [[2 * i + r for i in range(devices // 2)] for r in range(2)]
    mine = everywhere(mine.astype(f16), "gz", both)
    pairs = [keep[i] + given[i] for i in range(cols // 2)]
    pieces = pairs[:1] + [exchanged(2 * i, pairs[i]) for i in range(1, cols // 2)]
    input_grad = sum(pieces[1:], pieces[0]).astype(bf16)
    mine, input_grad = lax.optimization_barrier((mine, input_grad))
    beside = xor(mine, 1)
    scale = float((cells * devices) ** -0.5)

    def kernel(*refs):
        join_kernel(scale, *refs)

    filter_grad = call(
        kernel,
        jax.ShapeDtypeStruct((3, size, channels), f32),
        [],
        0,
        info,
        mine.astype(f32),
        beside.astype(f32),
    )
    return output[None], input_grad[None], filter_grad.reshape(3, 3, 3, local, channels)


def solution(mesh):
    in_specs = (P("gz", "col", None), P(None, None, None, "col", None), P("gz", "col", None))
    out_specs = (P("gz", "col", None), P("gz", "col", None), P(None, None, None, "col", None))
    return jax.shard_map(body, mesh=mesh, in_specs=in_specs, out_specs=out_specs, check_vma=False)
```

```python
import functools

import jax
import jax.numpy as jnp
from jax import lax
from jax.experimental import pallas as pl
from jax.experimental.pallas import tpu as pltpu
from jax.sharding import PartitionSpec as P

NY = 32
NZ = 16
VMEM = pl.BlockSpec(memory_space=pltpu.VMEM)
SMEM = pl.BlockSpec(memory_space=pltpu.SMEM)
ANY = pl.BlockSpec(memory_space=pl.ANY)
LOG2 = 0.6931471805599453
TOP = 13.0
EXTRA = 8
LANES = 128


def shifted(value, down, right):
    cells = NY * NZ
    step = down * NZ + right
    if step:
        value = pltpu.roll(value, (-step) % cells, 1)
    cell = lax.broadcasted_iota(jnp.int32, value.shape, 1)
    row, col = cell // NZ, cell % NZ
    if down == 1:
        value = jnp.where(row < NY - 1, value, 0.0)
    if down == -1:
        value = jnp.where(row > 0, value, 0.0)
    if right == 1:
        value = jnp.where(col < NZ - 1, value, 0.0)
    if right == -1:
        value = jnp.where(col > 0, value, 0.0)
    return value


def spread_taps(cot_ref, out_ref):
    outs = cot_ref.shape[0]
    wide = cot_ref[...].astype(jnp.float32)
    for tap in range(9):
        b, c = divmod(tap, 3)
        out_ref[tap * outs : (tap + 1) * outs, :] = shifted(wide, 1 - b, 1 - c).astype(jnp.bfloat16)


def lines(ref, first, count, beyond=False):
    _, both, cells = ref.shape
    local = both // 2
    start = local if beyond else 0
    return ref[pl.ds(first, count), start : start + local, :].reshape(count * local, cells)


def pack_kernel(own_ref, halo_ref, out_ref):
    blocks, both, _ = out_ref.shape
    local = both // 2
    for block in range(blocks):
        out_ref[block, :local, :] = own_ref[...]
        out_ref[block, local:, :] = halo_ref[...]


def input_kernel(info_ref, here_ref, there_ref, taps_ref, give_ref, keep_ref, spread_ref, acc_ref):
    away = 2 - 2 * (info_ref[0] % 2)
    spread_taps(here_ref.at[0], spread_ref.at[0])
    spread_taps(here_ref.at[1], spread_ref.at[1])
    spread_taps(there_ref.at[0], spread_ref.at[2])

    def part(a, source):
        return lax.dot_general(
            taps_ref[a], spread_ref[source], (((0,), (0,)), ((), ())), preferred_element_type=jnp.float32
        )

    acc_ref[...] = part(1, 0)
    acc_ref[...] += part(2 - away, 2)

    @pl.when(info_ref[1] == 0)
    def _():
        acc_ref[...] += part(away, 1)

    count, local, _ = keep_ref.shape
    col = info_ref[3]
    for i in range(count):
        keep_ref[i] = acc_ref[pl.ds(pl.multiple_of((col ^ (2 * i)) * local, local), local), :]
        give_ref[i] = acc_ref[pl.ds(pl.multiple_of((col ^ (2 * i + 1)) * local, local), local), :]


def output_kernel(info_ref, mine_ref, other_ref, taps_ref, out_ref, acc_ref):
    away = 2 * (info_ref[0] % 2)
    cols = mine_ref.shape[0]
    acc_ref[...] = jnp.dot(taps_ref[1], lines(mine_ref, 0, cols), preferred_element_type=jnp.float32)
    acc_ref[...] += jnp.dot(taps_ref[2 - away], lines(other_ref, 0, cols), preferred_element_type=jnp.float32)

    @pl.when(info_ref[1] == 0)
    def _():
        acc_ref[...] += jnp.dot(taps_ref[away], lines(mine_ref, 0, cols, True), preferred_element_type=jnp.float32)

    outs = acc_ref.shape[0] // 9
    total = jnp.zeros((outs, NY * NZ), jnp.float32)
    for tap in range(9):
        b, c = divmod(tap, 3)
        total = total + shifted(acc_ref[tap * outs : (tap + 1) * outs, :], b - 1, c - 1)
    out_ref[...] = total.astype(jnp.bfloat16)


def exponent(value):
    top = jnp.max(jnp.max(jnp.abs(value), axis=1, keepdims=True), axis=0, keepdims=True)
    top = jnp.broadcast_to(jnp.maximum(top, 1e-30), (1, LANES))
    return jnp.floor(jnp.log(top) * (1.0 / LOG2))


def filter_kernel(info_ref, mine_ref, other_ref, here_ref, there_ref, out_ref, window_ref, far_ref, spread_ref, acc_ref):
    core, side = info_ref[0] % 2, info_ref[0] // 2
    turn = 2 * core + side
    cols = mine_ref.shape[0]
    half, quarter = cols // 2, cols // 4
    width = acc_ref.shape[1]
    edge = 2 * width // 3
    for slab, ref, beyond in (
        (1 + core, mine_ref, False),
        (2 - core, other_ref, False),
        (3 * core, mine_ref, True),
        (3 - 3 * core, other_ref, True),
    ):
        window_ref[slab + 1 - side, :edge, :] = lines(ref, core * half, half, beyond)
        window_ref[slab + side, edge:, :] = lines(ref, turn * quarter, quarter, beyond)
    zeros = jnp.zeros((edge, window_ref.shape[2]), window_ref.dtype)
    window_ref[4 * side, :edge, :] = zeros
    window_ref[4 - 4 * side, edge:, :] = zeros[: width - edge]

    @pl.when(info_ref[2] == 1)
    def _():
        window_ref[1 + 2 * side, :edge, :] = zeros

    inside = core + side == 1

    @pl.when(inside)
    def _():
        far_ref[...] = here_ref[2]

    @pl.when(jnp.logical_not(inside))
    def _():
        far_ref[...] = there_ref[2]

    for index, (at, cot_ref) in enumerate(
        (
            (side + 1 + core, here_ref.at[0]),
            (side + 3 * core, here_ref.at[1]),
            (side + 2 - core, there_ref.at[0]),
            (side + 3 - 3 * core, there_ref.at[1]),
            (4 - 4 * side, far_ref),
        )
    ):
        spread_taps(cot_ref, spread_ref)
        part = lax.dot_general(
            spread_ref[...], window_ref[at], (((1,), (1,)), ((), ())), preferred_element_type=jnp.float32
        )
        if index:
            acc_ref[...] += part
        else:
            acc_ref[...] = part
    level = exponent(acc_ref[...])
    factor = jnp.exp((TOP - level) * LOG2)
    blocks, height, _ = out_ref.shape
    tiles = width // LANES
    rows = (height - EXTRA) // tiles
    for block in range(blocks):
        for tile in range(tiles):
            part = acc_ref[block * rows : (block + 1) * rows, tile * LANES : (tile + 1) * LANES]
            out_ref[block, tile * rows : (tile + 1) * rows, :] = part * factor
        out_ref[block, height - EXTRA :, :] = jnp.broadcast_to(level, (EXTRA, LANES))


def sum_kernel(in_ref, out_ref):
    blocks, height, _ = in_ref.shape
    height = height - EXTRA
    total = jnp.zeros((height, LANES), jnp.float32)
    for block in range(blocks):
        total = total + in_ref[block, :height, :] * jnp.exp((in_ref[block, height : height + 1, :] - TOP) * LOG2)
    level = exponent(total)
    out_ref[:height, :] = total * jnp.exp((TOP - level) * LOG2)
    out_ref[height:, :] = jnp.broadcast_to(level, (EXTRA, LANES))


def join_kernel(scale, flip, count, info_ref, *refs):
    pieces, (out_ref, lines_ref, sems) = refs[: 2 * count], refs[-3:]
    core = info_ref[0] % 2
    blocks, height, _ = pieces[0].shape
    height = height - EXTRA
    tiles = 3 * out_ref.shape[2] // (4 * LANES)
    rows = height // tiles
    wide = 2 * tiles // 3
    copies = []
    for index in range(count):
        for z in range(blocks // 2):
            spot = index * (blocks // 2) + z
            for its_core, piece_ref in ((core, pieces[index]), (1 - core, pieces[count + index])):
                for side in range(2):
                    block = 2 * z + side
                    down = jnp.exp((piece_ref[block, height : height + 1, :] - TOP) * LOG2) * scale
                    for tile in range(tiles):
                        value = piece_ref[block, tile * rows : (tile + 1) * rows, :] * down
                        if tile < wide:
                            offset, at = 2 * side, its_core * wide + tile
                        else:
                            offset, at = 1, (2 * its_core + side) * (tiles - wide) + tile - wide
                        lines_ref[spot, offset, :, pl.ds(pl.multiple_of(at * LANES, LANES), LANES)] = value
            first = (2 * spot + (1 - info_ref[4] if flip else info_ref[4])) * rows
            for offset in range(3):
                copy = pltpu.make_async_copy(
                    lines_ref.at[spot, offset],
                    out_ref.at[offset, pl.ds(pl.multiple_of(first, 8), rows), :],
                    sems.at[spot, offset],
                )
                copy.start()
                copies.append(copy)
    for copy in copies:
        copy.wait()


def call(kernel, out, scratch, flops, *args, into=None, spaces=VMEM):
    held = [] if into is None else [into]
    return pl.pallas_call(
        kernel,
        out_shape=out,
        in_specs=[SMEM if a.dtype == jnp.int32 else VMEM for a in args] + [ANY] * len(held),
        out_specs=[spaces] * len(out) if isinstance(out, list) else spaces,
        scratch_shapes=scratch,
        input_output_aliases={len(args): 0} if held else {},
        compiler_params=pltpu.CompilerParams(vmem_limit_bytes=12 << 20),
        cost_estimate=pl.CostEstimate(
            flops=flops, transcendentals=0, bytes_accessed=sum(a.size * a.dtype.itemsize for a in args)
        ),
    )(*args, *held)


def body(features, filters, cotangent):
    _, local, cells = features.shape
    devices = lax.axis_size("gz")
    cols = lax.axis_size("col")
    channels = local * cols
    quads = devices // 4
    half = channels // 2
    quarter = channels // 4
    size = 9 * local
    width = half + quarter
    height = size // quads * (width // LANES) + EXTRA
    flops = 2 * 27 * local * channels * cells
    bf16, f16, f32 = jnp.bfloat16, jnp.float16, jnp.float32
    place = lax.axis_index("gz")
    last = devices - 1
    info = jnp.stack(
        [
            place % 4,
            ((place == 0) | (place == last)).astype(jnp.int32),
            ((place < 2) | (place > last - 2)).astype(jnp.int32),
            lax.axis_index("col"),
            place // 4 % 2,
        ]
    ).astype(jnp.int32)
    x_own = features[0]
    c_own = cotangent[0]
    taps = filters.reshape(3, size, channels)

    def xor(value, bits):
        return lax.ppermute(value, "gz", [(i, i ^ bits) for i in range(devices)])

    outward = [(i, (i + 1) % devices if i % 2 else (i - 1) % devices) for i in range(devices)]
    ring = [[4 * g + r for g in range(quads)] for r in range(4)]

    def everywhere(block, axis, groups=None):
        count = len(groups[0]) if groups else lax.axis_size(axis)
        copies = jnp.broadcast_to(block[None], (count,) + block.shape)
        return lax.all_to_all(copies, axis, 0, 0, axis_index_groups=groups, tiled=True)

    x_halo = lax.ppermute(x_own, "gz", outward)
    c_halo = lax.ppermute(c_own, "gz", outward)
    across = xor(c_own, 2)
    x_halo, c_halo, across = lax.optimization_barrier((x_halo, c_halo, across))
    send = call(
        pack_kernel,
        jax.ShapeDtypeStruct((cols, 2 * local, cells), bf16),
        [],
        0,
        x_own,
        x_halo,
    )
    gathered = lax.all_to_all(send, "col", 0, 0, tiled=True)
    send, here = lax.optimization_barrier((send, jnp.stack([c_own, c_halo, across])))
    there = xor(here, 1)

    give, keep = call(
        input_kernel,
        [jax.ShapeDtypeStruct((cols // 2, local, cells), f32)] * 2,
        [pltpu.VMEM((3, size, cells), bf16), pltpu.VMEM((channels, cells), f32)],
        flops,
        info,
        here,
        there,
        taps,
    )
    gathered, there, give, keep = lax.optimization_barrier((gathered, there, give, keep))
    other = xor(gathered, 1)

    grads = call(
        filter_kernel,
        jax.ShapeDtypeStruct((quads, height, LANES), f32),
        [
            pltpu.VMEM((5, width, cells), bf16),
            pltpu.VMEM((local, cells), bf16),
            pltpu.VMEM((size, cells), bf16),
            pltpu.VMEM((size, width), f32),
        ],
        flops,
        info,
        gathered,
        other,
        here,
        there,
    )
    grads, other = lax.optimization_barrier((grads, other))
    narrow = lax.all_to_all(grads.astype(f16), "gz", 0, 0, axis_index_groups=ring, tiled=True)

    def exchanged(bits, value):
        return lax.ppermute(value, "col", [(j, j ^ bits) for j in range(cols)])

    given = exchanged(1, give)
    pairs = [keep[i] + given[i] for i in range(cols // 2)]
    pieces = pairs[:1] + [exchanged(2 * i, pairs[i]) for i in range(1, cols // 2)]
    other, _ = lax.optimization_barrier((other, given))
    narrow, pieces, other = lax.optimization_barrier((narrow, pieces, other))
    input_grad = sum(pieces[1:], pieces[0]).astype(bf16)
    output = call(
        output_kernel,
        jax.ShapeDtypeStruct((local, cells), bf16),
        [pltpu.VMEM((size, cells), f32)],
        flops,
        info,
        gathered,
        other,
        taps,
    )
    mine = call(
        sum_kernel,
        jax.ShapeDtypeStruct((height, LANES), f32),
        [],
        0,
        narrow.astype(f32),
    )
    every = [[8 * g + 4 * q + 2 * y + r for g in range(quads // 2) for y in range(2)] for q in range(2) for r in range(2)]
    mine = everywhere(mine.astype(f16), "gz", every)
    mine, output, input_grad = lax.optimization_barrier((mine, output, input_grad))
    first, second = mine[:quads // 2], mine[quads // 2 :]
    first = lax.ppermute(first, "gz", [(i, (i + 4) % devices) for i in range(devices)])
    second = lax.ppermute(second, "gz", [(i, (i - 4) % devices) for i in range(devices)])
    beside = xor(mine, 1)
    scale = float((cells * devices) ** -0.5)
    shape = jax.ShapeDtypeStruct((3, size, channels), f32)
    scratch = [pltpu.VMEM((quads // 2, 3, size // quads, channels), f32), pltpu.SemaphoreType.DMA((quads // 2, 3))]
    joined = call(
        functools.partial(join_kernel, scale, False, 1),
        shape,
        scratch,
        0,
        info,
        mine.astype(f32),
        beside.astype(f32),
        spaces=ANY,
    )
    joined, first, second = lax.optimization_barrier((joined, first, second))
    others = xor(first, 1), xor(second, 1)
    filter_grad = call(
        functools.partial(join_kernel, scale, True, 2),
        shape,
        scratch,
        0,
        info,
        first.astype(f32),
        second.astype(f32),
        others[0].astype(f32),
        others[1].astype(f32),
        into=joined,
        spaces=ANY,
    )
    return output[None], input_grad[None], filter_grad.reshape(3, 3, 3, local, channels)


def solution(mesh):
    in_specs = (P("gz", "col", None), P(None, None, None, "col", None), P("gz", "col", None))
    out_specs = (P("gz", "col", None), P("gz", "col", None), P(None, None, None, "col", None))
    return jax.shard_map(body, mesh=mesh, in_specs=in_specs, out_specs=out_specs, check_vma=False)
```

```python
import functools

import jax
import jax.numpy as jnp
from jax import lax
from jax.experimental import pallas as pl
from jax.experimental.pallas import tpu as pltpu
from jax.sharding import PartitionSpec as P

NY = 32
NZ = 16
VMEM = pl.BlockSpec(memory_space=pltpu.VMEM)
SMEM = pl.BlockSpec(memory_space=pltpu.SMEM)
ANY = pl.BlockSpec(memory_space=pl.ANY)
LOG2 = 0.6931471805599453
TOP = 13.0
EXTRA = 8
LANES = 128


def shifted(value, down, right):
    cells = NY * NZ
    step = down * NZ + right
    if step:
        value = pltpu.roll(value, (-step) % cells, 1)
    cell = lax.broadcasted_iota(jnp.int32, value.shape, 1)
    row, col = cell // NZ, cell % NZ
    if down == 1:
        value = jnp.where(row < NY - 1, value, 0.0)
    if down == -1:
        value = jnp.where(row > 0, value, 0.0)
    if right == 1:
        value = jnp.where(col < NZ - 1, value, 0.0)
    if right == -1:
        value = jnp.where(col > 0, value, 0.0)
    return value


def spread_taps(cot_ref, out_ref):
    outs = cot_ref.shape[0]
    wide = cot_ref[...].astype(jnp.float32)
    for tap in range(9):
        b, c = divmod(tap, 3)
        out_ref[tap * outs : (tap + 1) * outs, :] = shifted(wide, 1 - b, 1 - c).astype(jnp.bfloat16)


def lines(ref, first, count, beyond=False):
    _, both, cells = ref.shape
    local = both // 2
    start = local if beyond else 0
    return ref[pl.ds(first, count), start : start + local, :].reshape(count * local, cells)


def pack_kernel(part, in_ref, *refs):
    out_ref, sems = refs[-2:]
    blocks, both, _ = out_ref.shape
    local = both // 2
    copies = [
        pltpu.make_async_copy(in_ref, out_ref.at[block, pl.ds(part * local, local), :], sems.at[block])
        for block in range(blocks)
    ]
    for copy in copies:
        copy.start()
    for copy in copies:
        copy.wait()


def input_kernel(info_ref, here_ref, there_ref, taps_ref, give_ref, keep_ref, spread_ref, acc_ref):
    away = 2 - 2 * (info_ref[0] % 2)
    spread_taps(here_ref.at[0], spread_ref.at[0])
    spread_taps(here_ref.at[1], spread_ref.at[1])
    spread_taps(there_ref.at[0], spread_ref.at[2])

    def part(a, source):
        return lax.dot_general(
            taps_ref[a], spread_ref[source], (((0,), (0,)), ((), ())), preferred_element_type=jnp.float32
        )

    acc_ref[...] = part(1, 0)
    acc_ref[...] += part(2 - away, 2)

    @pl.when(info_ref[1] == 0)
    def _():
        acc_ref[...] += part(away, 1)

    count, local, _ = keep_ref.shape
    col = info_ref[3]
    for i in range(count):
        keep_ref[i] = acc_ref[pl.ds(pl.multiple_of((col ^ (2 * i)) * local, local), local), :]
        give_ref[i] = acc_ref[pl.ds(pl.multiple_of((col ^ (2 * i + 1)) * local, local), local), :]


def output_kernel(info_ref, mine_ref, other_ref, taps_ref, out_ref, acc_ref):
    away = 2 * (info_ref[0] % 2)
    cols = mine_ref.shape[0]
    acc_ref[...] = jnp.dot(taps_ref[1], lines(mine_ref, 0, cols), preferred_element_type=jnp.float32)
    acc_ref[...] += jnp.dot(taps_ref[2 - away], lines(other_ref, 0, cols), preferred_element_type=jnp.float32)

    @pl.when(info_ref[1] == 0)
    def _():
        acc_ref[...] += jnp.dot(taps_ref[away], lines(mine_ref, 0, cols, True), preferred_element_type=jnp.float32)

    outs = acc_ref.shape[0] // 9
    total = jnp.zeros((outs, NY * NZ), jnp.float32)
    for tap in range(9):
        b, c = divmod(tap, 3)
        total = total + shifted(acc_ref[tap * outs : (tap + 1) * outs, :], b - 1, c - 1)
    out_ref[...] = total.astype(jnp.bfloat16)


def exponent(value):
    top = jnp.max(jnp.max(jnp.abs(value), axis=1, keepdims=True), axis=0, keepdims=True)
    top = jnp.broadcast_to(jnp.maximum(top, 1e-30), (1, LANES))
    return jnp.floor(jnp.log(top) * (1.0 / LOG2))


def filter_kernel(info_ref, mine_ref, other_ref, here_ref, there_ref, out_ref, window_ref, far_ref, spread_ref, acc_ref):
    core, side = info_ref[0] % 2, info_ref[0] // 2
    turn = 2 * core + side
    cols = mine_ref.shape[0]
    half, quarter = cols // 2, cols // 4
    width = acc_ref.shape[1]
    edge = 2 * width // 3
    for slab, ref, beyond in (
        (1 + core, mine_ref, False),
        (2 - core, other_ref, False),
        (3 * core, mine_ref, True),
        (3 - 3 * core, other_ref, True),
    ):
        window_ref[slab + 1 - side, :edge, :] = lines(ref, core * half, half, beyond)
        window_ref[slab + side, edge:, :] = lines(ref, turn * quarter, quarter, beyond)
    zeros = jnp.zeros((edge, window_ref.shape[2]), window_ref.dtype)
    window_ref[4 * side, :edge, :] = zeros
    window_ref[4 - 4 * side, edge:, :] = zeros[: width - edge]

    @pl.when(info_ref[2] == 1)
    def _():
        window_ref[1 + 2 * side, :edge, :] = zeros

    inside = core + side == 1

    @pl.when(inside)
    def _():
        far_ref[...] = here_ref[2]

    @pl.when(jnp.logical_not(inside))
    def _():
        far_ref[...] = there_ref[2]

    for index, (at, cot_ref) in enumerate(
        (
            (side + 1 + core, here_ref.at[0]),
            (side + 3 * core, here_ref.at[1]),
            (side + 2 - core, there_ref.at[0]),
            (side + 3 - 3 * core, there_ref.at[1]),
            (4 - 4 * side, far_ref),
        )
    ):
        spread_taps(cot_ref, spread_ref)
        part = lax.dot_general(
            spread_ref[...], window_ref[at], (((1,), (1,)), ((), ())), preferred_element_type=jnp.float32
        )
        if index:
            acc_ref[...] += part
        else:
            acc_ref[...] = part
    level = exponent(acc_ref[...])
    factor = jnp.exp((TOP - level) * LOG2)
    blocks, height, _ = out_ref.shape
    tiles = width // LANES
    rows = (height - EXTRA) // tiles
    for block in range(blocks):
        for tile in range(tiles):
            part = acc_ref[block * rows : (block + 1) * rows, tile * LANES : (tile + 1) * LANES]
            out_ref[block, tile * rows : (tile + 1) * rows, :] = part * factor
        out_ref[block, height - EXTRA :, :] = jnp.broadcast_to(level, (EXTRA, LANES))


def sum_kernel(in_ref, out_ref):
    blocks, height, _ = in_ref.shape
    height = height - EXTRA
    total = jnp.zeros((height, LANES), jnp.float32)
    for block in range(blocks):
        total = total + in_ref[block, :height, :] * jnp.exp((in_ref[block, height : height + 1, :] - TOP) * LOG2)
    level = exponent(total)
    out_ref[:height, :] = total * jnp.exp((TOP - level) * LOG2)
    out_ref[height:, :] = jnp.broadcast_to(level, (EXTRA, LANES))


def join_kernel(scale, flip, count, info_ref, *refs):
    pieces, (out_ref, lines_ref, sems) = refs[: 2 * count], refs[-3:]
    core = info_ref[0] % 2
    blocks, height, _ = pieces[0].shape
    height = height - EXTRA
    tiles = 3 * out_ref.shape[2] // (4 * LANES)
    rows = height // tiles
    wide = 2 * tiles // 3
    copies = []
    for index in range(count):
        for z in range(blocks // 2):
            spot = index * (blocks // 2) + z
            for its_core, piece_ref in ((core, pieces[index]), (1 - core, pieces[count + index])):
                for side in range(2):
                    block = 2 * z + side
                    down = jnp.exp((piece_ref[block, height : height + 1, :] - TOP) * LOG2) * scale
                    for tile in range(tiles):
                        value = piece_ref[block, tile * rows : (tile + 1) * rows, :] * down
                        if tile < wide:
                            offset, at = 2 * side, its_core * wide + tile
                        else:
                            offset, at = 1, (2 * its_core + side) * (tiles - wide) + tile - wide
                        lines_ref[spot, offset, :, pl.ds(pl.multiple_of(at * LANES, LANES), LANES)] = value
            first = (2 * spot + (1 - info_ref[4] if flip else info_ref[4])) * rows
            for offset in range(3):
                copy = pltpu.make_async_copy(
                    lines_ref.at[spot, offset],
                    out_ref.at[offset, pl.ds(pl.multiple_of(first, 8), rows), :],
                    sems.at[spot, offset],
                )
                copy.start()
                copies.append(copy)
    for copy in copies:
        copy.wait()


def call(kernel, out, scratch, flops, *args, into=None, spaces=VMEM):
    held = [] if into is None else [into]
    return pl.pallas_call(
        kernel,
        out_shape=out,
        in_specs=[SMEM if a.dtype == jnp.int32 else VMEM for a in args] + [ANY] * len(held),
        out_specs=[spaces] * len(out) if isinstance(out, list) else spaces,
        scratch_shapes=scratch,
        input_output_aliases={len(args): 0} if held else {},
        compiler_params=pltpu.CompilerParams(vmem_limit_bytes=12 << 20),
        cost_estimate=pl.CostEstimate(
            flops=flops, transcendentals=0, bytes_accessed=sum(a.size * a.dtype.itemsize for a in args)
        ),
    )(*args, *held)


def body(features, filters, cotangent):
    _, local, cells = features.shape
    devices = lax.axis_size("gz")
    cols = lax.axis_size("col")
    channels = local * cols
    quads = devices // 4
    half = channels // 2
    quarter = channels // 4
    size = 9 * local
    width = half + quarter
    height = size // quads * (width // LANES) + EXTRA
    flops = 2 * 27 * local * channels * cells
    bf16, f16, f32 = jnp.bfloat16, jnp.float16, jnp.float32
    place = lax.axis_index("gz")
    last = devices - 1
    info = jnp.stack(
        [
            place % 4,
            ((place == 0) | (place == last)).astype(jnp.int32),
            ((place < 2) | (place > last - 2)).astype(jnp.int32),
            lax.axis_index("col"),
            place // 4 % 2,
        ]
    ).astype(jnp.int32)
    x_own = features[0]
    c_own = cotangent[0]
    taps = filters.reshape(3, size, channels)

    def xor(value, bits):
        return lax.ppermute(value, "gz", [(i, i ^ bits) for i in range(devices)])

    outward = [(i, (i + 1) % devices if i % 2 else (i - 1) % devices) for i in range(devices)]
    ring = [[4 * g + r for g in range(quads)] for r in range(4)]

    def everywhere(block, axis, groups=None):
        count = len(groups[0]) if groups else lax.axis_size(axis)
        copies = jnp.broadcast_to(block[None], (count,) + block.shape)
        return lax.all_to_all(copies, axis, 0, 0, axis_index_groups=groups, tiled=True)

    x_halo = lax.ppermute(x_own, "gz", outward)
    c_halo = lax.ppermute(c_own, "gz", outward)
    across = xor(c_own, 2)
    shape = jax.ShapeDtypeStruct((cols, 2 * local, cells), bf16)
    scratch = [pltpu.SemaphoreType.DMA((cols,))]
    send = call(functools.partial(pack_kernel, 0), shape, scratch, 0, x_own, spaces=ANY)
    x_halo, c_halo, across, send = lax.optimization_barrier((x_halo, c_halo, across, send))
    send = call(functools.partial(pack_kernel, 1), shape, scratch, 0, x_halo, into=send, spaces=ANY)
    gathered = lax.all_to_all(send, "col", 0, 0, tiled=True)
    send, here = lax.optimization_barrier((send, jnp.stack([c_own, c_halo, across])))
    there = xor(here, 1)

    give, keep = call(
        input_kernel,
        [jax.ShapeDtypeStruct((cols // 2, local, cells), f32)] * 2,
        [pltpu.VMEM((3, size, cells), bf16), pltpu.VMEM((channels, cells), f32)],
        flops,
        info,
        here,
        there,
        taps,
    )
    gathered, there, give, keep = lax.optimization_barrier((gathered, there, give, keep))
    other = xor(gathered, 1)

    grads = call(
        filter_kernel,
        jax.ShapeDtypeStruct((quads, height, LANES), f32),
        [
            pltpu.VMEM((5, width, cells), bf16),
            pltpu.VMEM((local, cells), bf16),
            pltpu.VMEM((size, cells), bf16),
            pltpu.VMEM((size, width), f32),
        ],
        flops,
        info,
        gathered,
        other,
        here,
        there,
    )
    grads, other = lax.optimization_barrier((grads, other))
    narrow = lax.all_to_all(grads.astype(f16), "gz", 0, 0, axis_index_groups=ring, tiled=True)

    def exchanged(bits, value):
        return lax.ppermute(value, "col", [(j, j ^ bits) for j in range(cols)])

    given = exchanged(1, give)
    pairs = [keep[i] + given[i] for i in range(cols // 2)]
    pieces = pairs[:1] + [exchanged(2 * i, pairs[i]) for i in range(1, cols // 2)]
    other, _ = lax.optimization_barrier((other, given))
    narrow, pieces, other = lax.optimization_barrier((narrow, pieces, other))
    input_grad = sum(pieces[1:], pieces[0]).astype(bf16)
    output = call(
        output_kernel,
        jax.ShapeDtypeStruct((local, cells), bf16),
        [pltpu.VMEM((size, cells), f32)],
        flops,
        info,
        gathered,
        other,
        taps,
    )
    mine = call(
        sum_kernel,
        jax.ShapeDtypeStruct((height, LANES), f32),
        [],
        0,
        narrow.astype(f32),
    )
    every = [[8 * g + 4 * q + 2 * y + r for g in range(quads // 2) for y in range(2)] for q in range(2) for r in range(2)]
    mine = everywhere(mine.astype(f16), "gz", every)
    mine, output, input_grad = lax.optimization_barrier((mine, output, input_grad))
    first, second = mine[:quads // 2], mine[quads // 2 :]
    first = lax.ppermute(first, "gz", [(i, (i + 4) % devices) for i in range(devices)])
    second = lax.ppermute(second, "gz", [(i, (i - 4) % devices) for i in range(devices)])
    beside = xor(mine, 1)
    scale = float((cells * devices) ** -0.5)
    shape = jax.ShapeDtypeStruct((3, size, channels), f32)
    scratch = [pltpu.VMEM((quads // 2, 3, size // quads, channels), f32), pltpu.SemaphoreType.DMA((quads // 2, 3))]
    joined = call(
        functools.partial(join_kernel, scale, False, 1),
        shape,
        scratch,
        0,
        info,
        mine.astype(f32),
        beside.astype(f32),
        spaces=ANY,
    )
    joined, first, second = lax.optimization_barrier((joined, first, second))
    others = xor(first, 1), xor(second, 1)
    filter_grad = call(
        functools.partial(join_kernel, scale, True, 2),
        shape,
        scratch,
        0,
        info,
        first.astype(f32),
        second.astype(f32),
        others[0].astype(f32),
        others[1].astype(f32),
        into=joined,
        spaces=ANY,
    )
    return output[None], input_grad[None], filter_grad.reshape(3, 3, 3, local, channels)


def solution(mesh):
    in_specs = (P("gz", "col", None), P(None, None, None, "col", None), P("gz", "col", None))
    out_specs = (P("gz", "col", None), P("gz", "col", None), P(None, None, None, "col", None))
    return jax.shard_map(body, mesh=mesh, in_specs=in_specs, out_specs=out_specs, check_vma=False)
```

```python
import functools

import jax
import jax.numpy as jnp
from jax import lax
from jax.experimental import pallas as pl
from jax.experimental.pallas import tpu as pltpu
from jax.sharding import PartitionSpec as P

NY = 32
NZ = 16
VMEM = pl.BlockSpec(memory_space=pltpu.VMEM)
SMEM = pl.BlockSpec(memory_space=pltpu.SMEM)
ANY = pl.BlockSpec(memory_space=pl.ANY)
LOG2 = 0.6931471805599453
TOP = 13.0
EXTRA = 8
LANES = 128


def shifted(value, down, right):
    cells = NY * NZ
    step = down * NZ + right
    if step:
        value = pltpu.roll(value, (-step) % cells, 1)
    cell = lax.broadcasted_iota(jnp.int32, value.shape, 1)
    row, col = cell // NZ, cell % NZ
    if down == 1:
        value = jnp.where(row < NY - 1, value, 0.0)
    if down == -1:
        value = jnp.where(row > 0, value, 0.0)
    if right == 1:
        value = jnp.where(col < NZ - 1, value, 0.0)
    if right == -1:
        value = jnp.where(col > 0, value, 0.0)
    return value


def spread_taps(cot_ref, out_ref):
    outs = cot_ref.shape[0]
    wide = cot_ref[...].astype(jnp.float32)
    for tap in range(9):
        b, c = divmod(tap, 3)
        out_ref[tap * outs : (tap + 1) * outs, :] = shifted(wide, 1 - b, 1 - c).astype(jnp.bfloat16)


def lines(ref, first, count, beyond=False):
    _, both, cells = ref.shape
    local = both // 2
    start = local if beyond else 0
    return ref[pl.ds(first, count), start : start + local, :].reshape(count * local, cells)


def pack_kernel(part, in_ref, *refs):
    out_ref, sems = refs[-2:]
    blocks, both, _ = out_ref.shape
    local = both // 2
    copies = [
        pltpu.make_async_copy(in_ref, out_ref.at[block, pl.ds(part * local, local), :], sems.at[block])
        for block in range(blocks)
    ]
    for copy in copies:
        copy.start()
    for copy in copies:
        copy.wait()


def input_kernel(info_ref, here_ref, there_ref, taps_ref, give_ref, keep_ref, spread_ref, acc_ref):
    away = 2 - 2 * (info_ref[0] % 2)
    spread_taps(here_ref.at[0], spread_ref.at[0])
    spread_taps(here_ref.at[1], spread_ref.at[1])
    spread_taps(there_ref.at[0], spread_ref.at[2])

    def part(a, source):
        return lax.dot_general(
            taps_ref[a], spread_ref[source], (((0,), (0,)), ((), ())), preferred_element_type=jnp.float32
        )

    acc_ref[...] = part(1, 0)
    acc_ref[...] += part(2 - away, 2)

    @pl.when(info_ref[1] == 0)
    def _():
        acc_ref[...] += part(away, 1)

    count, local, _ = keep_ref.shape
    col = info_ref[3]
    for i in range(count):
        keep_ref[i] = acc_ref[pl.ds(pl.multiple_of((col ^ (2 * i)) * local, local), local), :]
        give_ref[i] = acc_ref[pl.ds(pl.multiple_of((col ^ (2 * i + 1)) * local, local), local), :]


def output_kernel(info_ref, mine_ref, other_ref, taps_ref, out_ref, acc_ref):
    away = 2 * (info_ref[0] % 2)
    cols = mine_ref.shape[0]
    acc_ref[...] = jnp.dot(taps_ref[1], lines(mine_ref, 0, cols), preferred_element_type=jnp.float32)
    acc_ref[...] += jnp.dot(taps_ref[2 - away], lines(other_ref, 0, cols), preferred_element_type=jnp.float32)

    @pl.when(info_ref[1] == 0)
    def _():
        acc_ref[...] += jnp.dot(taps_ref[away], lines(mine_ref, 0, cols, True), preferred_element_type=jnp.float32)

    outs = acc_ref.shape[0] // 9
    total = jnp.zeros((outs, NY * NZ), jnp.float32)
    for tap in range(9):
        b, c = divmod(tap, 3)
        total = total + shifted(acc_ref[tap * outs : (tap + 1) * outs, :], b - 1, c - 1)
    out_ref[...] = total.astype(jnp.bfloat16)


def exponent(value):
    top = jnp.max(jnp.max(jnp.abs(value), axis=1, keepdims=True), axis=0, keepdims=True)
    top = jnp.broadcast_to(jnp.maximum(top, 1e-30), (1, LANES))
    return jnp.floor(jnp.log(top) * (1.0 / LOG2))


def filter_kernel(info_ref, mine_ref, other_ref, here_ref, there_ref, out_ref, window_ref, far_ref, spread_ref, acc_ref):
    core, side = info_ref[0] % 2, info_ref[0] // 2
    turn = 2 * core + side
    cols = mine_ref.shape[0]
    half, quarter = cols // 2, cols // 4
    width = acc_ref.shape[1]
    edge = 2 * width // 3
    for slab, ref, beyond in (
        (1 + core, mine_ref, False),
        (2 - core, other_ref, False),
        (3 * core, mine_ref, True),
        (3 - 3 * core, other_ref, True),
    ):
        window_ref[slab + 1 - side, :edge, :] = lines(ref, core * half, half, beyond)
        window_ref[slab + side, edge:, :] = lines(ref, turn * quarter, quarter, beyond)
    zeros = jnp.zeros((edge, window_ref.shape[2]), window_ref.dtype)
    window_ref[4 * side, :edge, :] = zeros
    window_ref[4 - 4 * side, edge:, :] = zeros[: width - edge]

    @pl.when(info_ref[2] == 1)
    def _():
        window_ref[1 + 2 * side, :edge, :] = zeros

    inside = core + side == 1

    @pl.when(inside)
    def _():
        far_ref[...] = here_ref[2]

    @pl.when(jnp.logical_not(inside))
    def _():
        far_ref[...] = there_ref[2]

    for index, (at, cot_ref) in enumerate(
        (
            (side + 1 + core, here_ref.at[0]),
            (side + 3 * core, here_ref.at[1]),
            (side + 2 - core, there_ref.at[0]),
            (side + 3 - 3 * core, there_ref.at[1]),
            (4 - 4 * side, far_ref),
        )
    ):
        spread_taps(cot_ref, spread_ref)
        part = lax.dot_general(
            spread_ref[...], window_ref[at], (((1,), (1,)), ((), ())), preferred_element_type=jnp.float32
        )
        if index:
            acc_ref[...] += part
        else:
            acc_ref[...] = part
    level = exponent(acc_ref[...])
    factor = jnp.exp((TOP - level) * LOG2)
    blocks, height, _ = out_ref.shape
    tiles = width // LANES
    rows = (height - EXTRA) // tiles
    for block in range(blocks):
        for tile in range(tiles):
            part = acc_ref[block * rows : (block + 1) * rows, tile * LANES : (tile + 1) * LANES]
            out_ref[block, tile * rows : (tile + 1) * rows, :] = part * factor
        out_ref[block, height - EXTRA :, :] = jnp.broadcast_to(level, (EXTRA, LANES))


def sum_kernel(in_ref, out_ref):
    blocks, height, _ = in_ref.shape
    height = height - EXTRA
    total = jnp.zeros((height, LANES), jnp.float32)
    for block in range(blocks):
        total = total + in_ref[block, :height, :] * jnp.exp((in_ref[block, height : height + 1, :] - TOP) * LOG2)
    level = exponent(total)
    out_ref[:height, :] = total * jnp.exp((TOP - level) * LOG2)
    out_ref[height:, :] = jnp.broadcast_to(level, (EXTRA, LANES))


def join_kernel(scale, flip, count, info_ref, *refs):
    pieces, (out_ref, lines_ref, sems) = refs[: 2 * count], refs[-3:]
    core = info_ref[0] % 2
    blocks, height, _ = pieces[0].shape
    height = height - EXTRA
    tiles = 3 * out_ref.shape[2] // (4 * LANES)
    rows = height // tiles
    wide = 2 * tiles // 3
    copies = []
    for index in range(count):
        for z in range(blocks // 2):
            spot = index * (blocks // 2) + z
            for its_core, piece_ref in ((core, pieces[index]), (1 - core, pieces[count + index])):
                for side in range(2):
                    block = 2 * z + side
                    down = jnp.exp((piece_ref[block, height : height + 1, :] - TOP) * LOG2) * scale
                    for tile in range(tiles):
                        value = piece_ref[block, tile * rows : (tile + 1) * rows, :] * down
                        if tile < wide:
                            offset, at = 2 * side, its_core * wide + tile
                        else:
                            offset, at = 1, (2 * its_core + side) * (tiles - wide) + tile - wide
                        lines_ref[spot, offset, :, pl.ds(pl.multiple_of(at * LANES, LANES), LANES)] = value
            first = (2 * spot + (1 - info_ref[4] if flip else info_ref[4])) * rows
            for offset in range(3):
                copy = pltpu.make_async_copy(
                    lines_ref.at[spot, offset],
                    out_ref.at[offset, pl.ds(pl.multiple_of(first, 8), rows), :],
                    sems.at[spot, offset],
                )
                copy.start()
                copies.append(copy)
    for copy in copies:
        copy.wait()


def call(kernel, out, scratch, flops, *args, into=None, spaces=VMEM):
    held = [] if into is None else [into]
    return pl.pallas_call(
        kernel,
        out_shape=out,
        in_specs=[SMEM if a.dtype == jnp.int32 else VMEM for a in args] + [ANY] * len(held),
        out_specs=[spaces] * len(out) if isinstance(out, list) else spaces,
        scratch_shapes=scratch,
        input_output_aliases={len(args): 0} if held else {},
        compiler_params=pltpu.CompilerParams(vmem_limit_bytes=12 << 20),
        cost_estimate=pl.CostEstimate(
            flops=flops, transcendentals=0, bytes_accessed=sum(a.size * a.dtype.itemsize for a in args)
        ),
    )(*args, *held)


def body(features, filters, cotangent):
    _, local, cells = features.shape
    devices = lax.axis_size("gz")
    cols = lax.axis_size("col")
    channels = local * cols
    quads = devices // 4
    half = channels // 2
    quarter = channels // 4
    size = 9 * local
    width = half + quarter
    height = size // quads * (width // LANES) + EXTRA
    flops = 2 * 27 * local * channels * cells
    bf16, f16, f32 = jnp.bfloat16, jnp.float16, jnp.float32
    place = lax.axis_index("gz")
    last = devices - 1
    info = jnp.stack(
        [
            place % 4,
            ((place == 0) | (place == last)).astype(jnp.int32),
            ((place < 2) | (place > last - 2)).astype(jnp.int32),
            lax.axis_index("col"),
            place // 4 % 2,
        ]
    ).astype(jnp.int32)
    x_own = features[0]
    c_own = cotangent[0]
    taps = filters.reshape(3, size, channels)

    def xor(value, bits):
        return lax.ppermute(value, "gz", [(i, i ^ bits) for i in range(devices)])

    outward = [(i, (i + 1) % devices if i % 2 else (i - 1) % devices) for i in range(devices)]
    ring = [[4 * g + r for g in range(quads)] for r in range(4)]

    def everywhere(block, axis, groups=None):
        count = len(groups[0]) if groups else lax.axis_size(axis)
        copies = jnp.broadcast_to(block[None], (count,) + block.shape)
        return lax.all_to_all(copies, axis, 0, 0, axis_index_groups=groups, tiled=True)

    x_halo = lax.ppermute(x_own, "gz", outward)
    c_halo = lax.ppermute(c_own, "gz", outward)
    inward = [(4 * g + 3 * r, 4 * g + 2 - r) for g in range(quads) for r in range(2)]
    across = lax.ppermute(c_own, "gz", inward)
    shape = jax.ShapeDtypeStruct((cols, 2 * local, cells), bf16)
    scratch = [pltpu.SemaphoreType.DMA((cols,))]
    send = call(functools.partial(pack_kernel, 0), shape, scratch, 0, x_own, spaces=ANY)
    x_halo, c_halo, across, send = lax.optimization_barrier((x_halo, c_halo, across, send))
    send = call(functools.partial(pack_kernel, 1), shape, scratch, 0, x_halo, into=send, spaces=ANY)
    gathered = lax.all_to_all(send, "col", 0, 0, tiled=True)
    send, here = lax.optimization_barrier((send, jnp.stack([c_own, c_halo, across])))
    there = xor(here, 1)

    give, keep = call(
        input_kernel,
        [jax.ShapeDtypeStruct((cols // 2, local, cells), f32)] * 2,
        [pltpu.VMEM((3, size, cells), bf16), pltpu.VMEM((channels, cells), f32)],
        flops,
        info,
        here,
        there,
        taps,
    )
    gathered, there, give, keep = lax.optimization_barrier((gathered, there, give, keep))
    other = xor(gathered, 1)

    grads = call(
        filter_kernel,
        jax.ShapeDtypeStruct((quads, height, LANES), f32),
        [
            pltpu.VMEM((5, width, cells), bf16),
            pltpu.VMEM((local, cells), bf16),
            pltpu.VMEM((size, cells), bf16),
            pltpu.VMEM((size, width), f32),
        ],
        flops,
        info,
        gathered,
        other,
        here,
        there,
    )
    grads, other = lax.optimization_barrier((grads, other))
    narrow = lax.all_to_all(grads.astype(f16), "gz", 0, 0, axis_index_groups=ring, tiled=True)

    def exchanged(bits, value):
        return lax.ppermute(value, "col", [(j, j ^ bits) for j in range(cols)])

    given = exchanged(1, give)
    pairs = [keep[i] + given[i] for i in range(cols // 2)]
    pieces = pairs[:1] + [exchanged(2 * i, pairs[i]) for i in range(1, cols // 2)]
    other, _ = lax.optimization_barrier((other, given))
    narrow, pieces, other = lax.optimization_barrier((narrow, pieces, other))
    input_grad = sum(pieces[1:], pieces[0]).astype(bf16)
    output = call(
        output_kernel,
        jax.ShapeDtypeStruct((local, cells), bf16),
        [pltpu.VMEM((size, cells), f32)],
        flops,
        info,
        gathered,
        other,
        taps,
    )
    mine = call(
        sum_kernel,
        jax.ShapeDtypeStruct((height, LANES), f32),
        [],
        0,
        narrow.astype(f32),
    )
    every = [[8 * g + 4 * q + 2 * y + r for g in range(quads // 2) for y in range(2)] for q in range(2) for r in range(2)]
    mine = everywhere(mine.astype(f16), "gz", every)
    mine, output, input_grad = lax.optimization_barrier((mine, output, input_grad))
    first, second = mine[:quads // 2], mine[quads // 2 :]
    first = lax.ppermute(first, "gz", [(i, (i + 4) % devices) for i in range(devices)])
    second = lax.ppermute(second, "gz", [(i, (i - 4) % devices) for i in range(devices)])
    beside = xor(mine, 1)
    scale = float((cells * devices) ** -0.5)
    shape = jax.ShapeDtypeStruct((3, size, channels), f32)
    scratch = [pltpu.VMEM((quads // 2, 3, size // quads, channels), f32), pltpu.SemaphoreType.DMA((quads // 2, 3))]
    joined = call(
        functools.partial(join_kernel, scale, False, 1),
        shape,
        scratch,
        0,
        info,
        mine.astype(f32),
        beside.astype(f32),
        spaces=ANY,
    )
    joined, first, second = lax.optimization_barrier((joined, first, second))
    others = xor(first, 1), xor(second, 1)
    filter_grad = call(
        functools.partial(join_kernel, scale, True, 2),
        shape,
        scratch,
        0,
        info,
        first.astype(f32),
        second.astype(f32),
        others[0].astype(f32),
        others[1].astype(f32),
        into=joined,
        spaces=ANY,
    )
    return output[None], input_grad[None], filter_grad.reshape(3, 3, 3, local, channels)


def solution(mesh):
    in_specs = (P("gz", "col", None), P(None, None, None, "col", None), P("gz", "col", None))
    out_specs = (P("gz", "col", None), P("gz", "col", None), P(None, None, None, "col", None))
    return jax.shard_map(body, mesh=mesh, in_specs=in_specs, out_specs=out_specs, check_vma=False)
```

```python
import functools

import jax
import jax.numpy as jnp
from jax import lax
from jax.experimental import pallas as pl
from jax.experimental.pallas import tpu as pltpu
from jax.sharding import PartitionSpec as P

NY = 32
NZ = 16
VMEM = pl.BlockSpec(memory_space=pltpu.VMEM)
SMEM = pl.BlockSpec(memory_space=pltpu.SMEM)
ANY = pl.BlockSpec(memory_space=pl.ANY)
LOG2 = 0.6931471805599453
TOP = 13.0
EXTRA = 8
LANES = 128


def shifted(value, down, right):
    cells = NY * NZ
    step = down * NZ + right
    if step:
        value = pltpu.roll(value, (-step) % cells, 1)
    cell = lax.broadcasted_iota(jnp.int32, value.shape, 1)
    row, col = cell // NZ, cell % NZ
    if down == 1:
        value = jnp.where(row < NY - 1, value, 0.0)
    if down == -1:
        value = jnp.where(row > 0, value, 0.0)
    if right == 1:
        value = jnp.where(col < NZ - 1, value, 0.0)
    if right == -1:
        value = jnp.where(col > 0, value, 0.0)
    return value


def spread_taps(cot_ref, out_ref):
    outs = cot_ref.shape[0]
    wide = cot_ref[...].astype(jnp.float32)
    for tap in range(9):
        b, c = divmod(tap, 3)
        out_ref[tap * outs : (tap + 1) * outs, :] = shifted(wide, 1 - b, 1 - c).astype(jnp.bfloat16)


def lines(ref, first, count, beyond=False):
    _, both, cells = ref.shape
    local = both // 2
    start = local if beyond else 0
    return ref[pl.ds(first, count), start : start + local, :].reshape(count * local, cells)


def pack_kernel(part, in_ref, *refs):
    out_ref, sems = refs[-2:]
    blocks, both, _ = out_ref.shape
    local = both // 2
    copies = [
        pltpu.make_async_copy(in_ref, out_ref.at[block, pl.ds(part * local, local), :], sems.at[block])
        for block in range(blocks)
    ]
    for copy in copies:
        copy.start()
    for copy in copies:
        copy.wait()


def input_kernel(info_ref, here_ref, there_ref, taps_ref, give_ref, keep_ref, spread_ref, acc_ref):
    away = 2 - 2 * (info_ref[0] % 2)
    spread_taps(here_ref.at[0], spread_ref.at[0])
    spread_taps(here_ref.at[1], spread_ref.at[1])
    spread_taps(there_ref.at[0], spread_ref.at[2])

    def part(a, source):
        return lax.dot_general(
            taps_ref[a], spread_ref[source], (((0,), (0,)), ((), ())), preferred_element_type=jnp.float32
        )

    acc_ref[...] = part(1, 0)
    acc_ref[...] += part(2 - away, 2)

    @pl.when(info_ref[1] == 0)
    def _():
        acc_ref[...] += part(away, 1)

    count, local, _ = keep_ref.shape
    col = info_ref[3]
    for i in range(count):
        keep_ref[i] = acc_ref[pl.ds(pl.multiple_of((col ^ (2 * i)) * local, local), local), :]
        give_ref[i] = acc_ref[pl.ds(pl.multiple_of((col ^ (2 * i + 1)) * local, local), local), :]


def output_kernel(info_ref, mine_ref, other_ref, taps_ref, out_ref, acc_ref):
    away = 2 * (info_ref[0] % 2)
    cols = mine_ref.shape[0]
    acc_ref[...] = jnp.dot(taps_ref[1], lines(mine_ref, 0, cols), preferred_element_type=jnp.float32)
    acc_ref[...] += jnp.dot(taps_ref[2 - away], lines(other_ref, 0, cols), preferred_element_type=jnp.float32)

    @pl.when(info_ref[1] == 0)
    def _():
        acc_ref[...] += jnp.dot(taps_ref[away], lines(mine_ref, 0, cols, True), preferred_element_type=jnp.float32)

    outs = acc_ref.shape[0] // 9
    total = jnp.zeros((outs, NY * NZ), jnp.float32)
    for tap in range(9):
        b, c = divmod(tap, 3)
        total = total + shifted(acc_ref[tap * outs : (tap + 1) * outs, :], b - 1, c - 1)
    out_ref[...] = total.astype(jnp.bfloat16)


def exponent(value):
    top = jnp.max(jnp.max(jnp.abs(value), axis=1, keepdims=True), axis=0, keepdims=True)
    top = jnp.broadcast_to(jnp.maximum(top, 1e-30), (1, LANES))
    return jnp.floor(jnp.log(top) * (1.0 / LOG2))


def filter_kernel(info_ref, mine_ref, other_ref, here_ref, there_ref, out_ref, window_ref, far_ref, spread_ref, acc_ref):
    core, side = info_ref[0] % 2, info_ref[0] // 2
    turn = 2 * core + side
    cols = mine_ref.shape[0]
    half, quarter = cols // 2, cols // 4
    width = acc_ref.shape[1]
    edge = 2 * width // 3
    for slab, ref, beyond in (
        (1 + core, mine_ref, False),
        (2 - core, other_ref, False),
        (3 * core, mine_ref, True),
        (3 - 3 * core, other_ref, True),
    ):
        window_ref[slab + 1 - side, :edge, :] = lines(ref, core * half, half, beyond)
        window_ref[slab + side, edge:, :] = lines(ref, turn * quarter, quarter, beyond)
    zeros = jnp.zeros((edge, window_ref.shape[2]), window_ref.dtype)
    window_ref[4 * side, :edge, :] = zeros
    window_ref[4 - 4 * side, edge:, :] = zeros[: width - edge]

    @pl.when(info_ref[2] == 1)
    def _():
        window_ref[1 + 2 * side, :edge, :] = zeros

    inside = core + side == 1

    @pl.when(inside)
    def _():
        far_ref[...] = here_ref[2]

    @pl.when(jnp.logical_not(inside))
    def _():
        far_ref[...] = there_ref[2]

    for index, (at, cot_ref) in enumerate(
        (
            (side + 1 + core, here_ref.at[0]),
            (side + 3 * core, here_ref.at[1]),
            (side + 2 - core, there_ref.at[0]),
            (side + 3 - 3 * core, there_ref.at[1]),
            (4 - 4 * side, far_ref),
        )
    ):
        spread_taps(cot_ref, spread_ref)
        part = lax.dot_general(
            spread_ref[...], window_ref[at], (((1,), (1,)), ((), ())), preferred_element_type=jnp.float32
        )
        if index:
            acc_ref[...] += part
        else:
            acc_ref[...] = part
    level = exponent(acc_ref[...])
    factor = jnp.exp((TOP - level) * LOG2)
    blocks, height, _ = out_ref.shape
    tiles = width // LANES
    rows = (height - EXTRA) // tiles
    for block in range(blocks):
        for tile in range(tiles):
            part = acc_ref[block * rows : (block + 1) * rows, tile * LANES : (tile + 1) * LANES]
            out_ref[block, tile * rows : (tile + 1) * rows, :] = part * factor
        out_ref[block, height - EXTRA :, :] = jnp.broadcast_to(level, (EXTRA, LANES))


def sum_kernel(in_ref, out_ref):
    blocks, height, _ = in_ref.shape
    height = height - EXTRA
    total = jnp.zeros((height, LANES), jnp.float32)
    for block in range(blocks):
        total = total + in_ref[block, :height, :] * jnp.exp((in_ref[block, height : height + 1, :] - TOP) * LOG2)
    level = exponent(total)
    out_ref[:height, :] = total * jnp.exp((TOP - level) * LOG2)
    out_ref[height:, :] = jnp.broadcast_to(level, (EXTRA, LANES))


def join_kernel(scale, flip, count, info_ref, *refs):
    pieces, (out_ref, lines_ref, sems) = refs[: 2 * count], refs[-3:]
    core = info_ref[0] % 2
    blocks, height, _ = pieces[0].shape
    height = height - EXTRA
    tiles = 3 * out_ref.shape[2] // (4 * LANES)
    rows = height // tiles
    wide = 2 * tiles // 3
    copies = []
    for index in range(count):
        for z in range(blocks // 2):
            spot = index * (blocks // 2) + z
            for its_core, piece_ref in ((core, pieces[index]), (1 - core, pieces[count + index])):
                for side in range(2):
                    block = 2 * z + side
                    down = jnp.exp((piece_ref[block, height : height + 1, :] - TOP) * LOG2) * scale
                    for tile in range(tiles):
                        value = piece_ref[block, tile * rows : (tile + 1) * rows, :] * down
                        if tile < wide:
                            offset, at = 2 * side, its_core * wide + tile
                        else:
                            offset, at = 1, (2 * its_core + side) * (tiles - wide) + tile - wide
                        lines_ref[spot, offset, :, pl.ds(pl.multiple_of(at * LANES, LANES), LANES)] = value
            first = (2 * spot + (1 - info_ref[4] if flip else info_ref[4])) * rows
            for offset in range(3):
                copy = pltpu.make_async_copy(
                    lines_ref.at[spot, offset],
                    out_ref.at[offset, pl.ds(pl.multiple_of(first, 8), rows), :],
                    sems.at[spot, offset],
                )
                copy.start()
                copies.append(copy)
    for copy in copies:
        copy.wait()


def call(kernel, out, scratch, flops, *args, into=None, spaces=VMEM):
    held = [] if into is None else [into]
    return pl.pallas_call(
        kernel,
        out_shape=out,
        in_specs=[SMEM if a.dtype == jnp.int32 else VMEM for a in args] + [ANY] * len(held),
        out_specs=[spaces] * len(out) if isinstance(out, list) else spaces,
        scratch_shapes=scratch,
        input_output_aliases={len(args): 0} if held else {},
        compiler_params=pltpu.CompilerParams(vmem_limit_bytes=12 << 20),
        cost_estimate=pl.CostEstimate(
            flops=flops, transcendentals=0, bytes_accessed=sum(a.size * a.dtype.itemsize for a in args)
        ),
    )(*args, *held)


def body(features, filters, cotangent):
    _, local, cells = features.shape
    devices = lax.axis_size("gz")
    cols = lax.axis_size("col")
    channels = local * cols
    quads = devices // 4
    half = channels // 2
    quarter = channels // 4
    size = 9 * local
    width = half + quarter
    height = size // quads * (width // LANES) + EXTRA
    flops = 2 * 27 * local * channels * cells
    bf16, f16, f32 = jnp.bfloat16, jnp.float16, jnp.float32
    place = lax.axis_index("gz")
    last = devices - 1
    info = jnp.stack(
        [
            place % 4,
            ((place == 0) | (place == last)).astype(jnp.int32),
            ((place < 2) | (place > last - 2)).astype(jnp.int32),
            lax.axis_index("col"),
            place // 4 % 2,
        ]
    ).astype(jnp.int32)
    x_own = features[0]
    c_own = cotangent[0]
    taps = filters.reshape(3, size, channels)

    def xor(value, bits):
        return lax.ppermute(value, "gz", [(i, i ^ bits) for i in range(devices)])

    outward = [(i, (i + 1) % devices if i % 2 else (i - 1) % devices) for i in range(devices)]
    ring = [[4 * g + r for g in range(quads)] for r in range(4)]

    def everywhere(block, axis, groups=None):
        count = len(groups[0]) if groups else lax.axis_size(axis)
        copies = jnp.broadcast_to(block[None], (count,) + block.shape)
        return lax.all_to_all(copies, axis, 0, 0, axis_index_groups=groups, tiled=True)

    x_halo = lax.ppermute(x_own, "gz", outward)
    c_halo = lax.ppermute(c_own, "gz", outward)
    across = xor(c_own, 2)
    shape = jax.ShapeDtypeStruct((cols, 2 * local, cells), bf16)
    scratch = [pltpu.SemaphoreType.DMA((cols,))]
    send = call(functools.partial(pack_kernel, 0), shape, scratch, 0, x_own, spaces=ANY)
    x_halo, c_halo, across, send = lax.optimization_barrier((x_halo, c_halo, across, send))
    send = call(functools.partial(pack_kernel, 1), shape, scratch, 0, x_halo, into=send, spaces=ANY)
    gathered = lax.all_to_all(send, "col", 0, 0, tiled=True)
    send, here = lax.optimization_barrier((send, jnp.stack([c_own, c_halo, across])))
    there = xor(here, 1)

    give, keep = call(
        input_kernel,
        [jax.ShapeDtypeStruct((cols // 2, local, cells), f32)] * 2,
        [pltpu.VMEM((3, size, cells), bf16), pltpu.VMEM((channels, cells), f32)],
        flops,
        info,
        here,
        there,
        taps,
    )
    gathered, there, give, keep = lax.optimization_barrier((gathered, there, give, keep))
    other = xor(gathered, 1)

    grads = call(
        filter_kernel,
        jax.ShapeDtypeStruct((quads, height, LANES), f32),
        [
            pltpu.VMEM((5, width, cells), bf16),
            pltpu.VMEM((local, cells), bf16),
            pltpu.VMEM((size, cells), bf16),
            pltpu.VMEM((size, width), f32),
        ],
        flops,
        info,
        gathered,
        other,
        here,
        there,
    )
    grads, other = lax.optimization_barrier((grads, other))
    narrow = lax.all_to_all(grads.astype(f16), "gz", 0, 0, axis_index_groups=ring, tiled=True)

    def exchanged(bits, value):
        return lax.ppermute(value, "col", [(j, j ^ bits) for j in range(cols)])

    given = exchanged(1, give)
    pairs = [keep[i] + given[i] for i in range(cols // 2)]
    pieces = pairs[:1] + [exchanged(2 * i, pairs[i]) for i in range(1, cols // 2)]
    other, _ = lax.optimization_barrier((other, given))
    near = [pieces[0]] + pieces[1::2]
    narrow, near, far, other = lax.optimization_barrier((narrow, near, pairs[2], other))
    pieces = near + [exchanged(4, far)]
    input_grad = sum(pieces[1:], pieces[0]).astype(bf16)
    output = call(
        output_kernel,
        jax.ShapeDtypeStruct((local, cells), bf16),
        [pltpu.VMEM((size, cells), f32)],
        flops,
        info,
        gathered,
        other,
        taps,
    )
    mine = call(
        sum_kernel,
        jax.ShapeDtypeStruct((height, LANES), f32),
        [],
        0,
        narrow.astype(f32),
    )
    every = [[8 * g + 4 * q + 2 * y + r for g in range(quads // 2) for y in range(2)] for q in range(2) for r in range(2)]
    mine = everywhere(mine.astype(f16), "gz", every)
    mine, output, input_grad = lax.optimization_barrier((mine, output, input_grad))
    first, second = mine[:quads // 2], mine[quads // 2 :]
    first = lax.ppermute(first, "gz", [(i, (i + 4) % devices) for i in range(devices)])
    second = lax.ppermute(second, "gz", [(i, (i - 4) % devices) for i in range(devices)])
    beside = xor(mine, 1)
    scale = float((cells * devices) ** -0.5)
    shape = jax.ShapeDtypeStruct((3, size, channels), f32)
    scratch = [pltpu.VMEM((quads // 2, 3, size // quads, channels), f32), pltpu.SemaphoreType.DMA((quads // 2, 3))]
    joined = call(
        functools.partial(join_kernel, scale, False, 1),
        shape,
        scratch,
        0,
        info,
        mine.astype(f32),
        beside.astype(f32),
        spaces=ANY,
    )
    joined, first, second = lax.optimization_barrier((joined, first, second))
    others = xor(first, 1), xor(second, 1)
    filter_grad = call(
        functools.partial(join_kernel, scale, True, 2),
        shape,
        scratch,
        0,
        info,
        first.astype(f32),
        second.astype(f32),
        others[0].astype(f32),
        others[1].astype(f32),
        into=joined,
        spaces=ANY,
    )
    return output[None], input_grad[None], filter_grad.reshape(3, 3, 3, local, channels)


def solution(mesh):
    in_specs = (P("gz", "col", None), P(None, None, None, "col", None), P("gz", "col", None))
    out_specs = (P("gz", "col", None), P("gz", "col", None), P(None, None, None, "col", None))
    return jax.shard_map(body, mesh=mesh, in_specs=in_specs, out_specs=out_specs, check_vma=False)
```
